256 devices in a mesh: blk: 16 (over y, z_lo, core), dp: 16 (over z_hi, x).
Axes of the slice: x: 4, y: 4, z: 8 (z_hi: 4, z_lo: 2; z = z_hi * 2 + z_lo), core: 2. Of those that a mesh axis runs over, the one named last changes fastest.
Arguments:
- queries: bfloat16 [32768, 256], P(('blk', 'dp')), may hold values from -30 to 30, as said below
- pois: bfloat16 [32768, 256], P(('blk', 'dp')), may hold values from -4 to 4, as said below
- query_region: int32 [32768], P(('blk', 'dp')), may hold values from 0 to 63
- block_region: int32 [256], P(('blk', 'dp')), may hold values from 0 to 63
- region_mask: int32 [64, 64], replicated, may hold values from 0 to 1
- positive: int32 [32768], P(('blk', 'dp')), may hold values from 0 to 32767
Outputs:
- loss: float32 [32768], P(('blk', 'dp'))
- query_grad: float32 [32768, 256], P(('blk', 'dp'))
- poi_grad: float32 [32768, 256], P(('blk', 'dp'))
The draws below stay inside these ranges and needn't reach their ends.
Inputs may be any that keep to these rules, and one draw needn't show every extreme that they name: `queries`: float entries. `pois`: float entries.
All inputs are finite; a program needn't handle non-finite values.
Results may differ from the reference program's by a relative error of at most 0.00185.
Values may be sent and summed in bfloat16 or wider, within the bound.
A program may use at most 64 MiB of HBM per device.

```python
import math
import jax
import jax.numpy as jnp
from jax import lax

E = 256
TILE = 128
R = 64
QUERIES = 32768
POIS = 32768
BLOCKS = 256


def poi_base(key):
    return jnp.clip(jax.random.normal(jax.random.fold_in(key, 11), (POIS, E), jnp.float32), -4.0, 4.0)


def query_regions(key):
    rows = jnp.arange(QUERIES, dtype=jnp.int32)
    jitter = jax.random.randint(jax.random.fold_in(key, 29), (QUERIES,), 0, 3, dtype=jnp.int32)
    values = (rows * R // QUERIES + jitter) % R
    values = values.at[0].set(0)
    return values.at[QUERIES - 1].set(R - 1)


def block_regions(key):
    rows = jnp.arange(BLOCKS, dtype=jnp.int32)
    jitter = jax.random.randint(jax.random.fold_in(key, 31), (BLOCKS,), 0, 3, dtype=jnp.int32)
    values = (rows * R // BLOCKS + jitter) % R
    values = values.at[0].set(0)
    return values.at[BLOCKS - 1].set(R - 1)


def region_table(key):
    first = jnp.arange(R, dtype=jnp.int32)[:, None]
    second = jnp.arange(R, dtype=jnp.int32)[None, :]
    offset = (second - first) % R
    distance = jnp.minimum(offset, R - offset)
    reach = jax.random.randint(jax.random.fold_in(key, 37), (R, 1), 1, R // 4 + 1, dtype=jnp.int32)
    extra = jax.random.randint(jax.random.fold_in(key, 41), (R, R), 0, 10, dtype=jnp.int32) == 0
    return ((distance < reach) | extra).astype(jnp.int32)


def positive_ids(key):
    owner = query_regions(key)
    kinds = block_regions(key)
    table = region_table(key)
    allowed = table[owner][:, kinds]
    noise = jax.random.randint(jax.random.fold_in(key, 13), (QUERIES, BLOCKS), 0, 1024, dtype=jnp.int32)
    index = jnp.arange(BLOCKS, dtype=jnp.int32)[None, :]
    score = allowed * (1024 * BLOCKS) + noise * BLOCKS + index
    chosen_block = lax.top_k(score, 1)[1][:, 0].astype(jnp.int32)
    within = jax.random.randint(jax.random.fold_in(key, 43), (QUERIES,), 0, TILE, dtype=jnp.int32)
    values = chosen_block * TILE + within
    values = values.at[0].set(0)
    return values.at[QUERIES - 1].set(POIS - 1)


def draw_positive(key, part):
    return positive_ids(key)


def draw_queries(key, part):
    values = jnp.clip(jax.random.normal(jax.random.fold_in(key, 17), (QUERIES, E), jnp.float32), -4.0, 4.0)
    return values.astype(jnp.bfloat16)


def draw_pois(key, part):
    base = poi_base(key)
    return base.astype(jnp.bfloat16)


def draw_query_region(key, part):
    return query_regions(key)


def draw_block_region(key, part):
    return block_regions(key)


def draw_region_mask(key, part):
    return region_table(key)


def setup_inputs(seed: int = 0) -> dict:
    key_of = jax.random.split(jax.random.key(seed), 7)
    return {
        "queries": draw_queries(jax.random.fold_in(key_of[6], 71), 0),
        "pois": draw_pois(jax.random.fold_in(key_of[6], 71), 0),
        "query_region": draw_query_region(jax.random.fold_in(key_of[6], 71), 0),
        "block_region": draw_block_region(jax.random.fold_in(key_of[6], 71), 0),
        "region_mask": draw_region_mask(jax.random.fold_in(key_of[6], 71), 0),
        "positive": draw_positive(jax.random.fold_in(key_of[6], 71), 0),
    }


floor_value = -1e+30

def reference(queries, pois, query_region, block_region, region_mask, positive):
    scale = 1.0 / math.sqrt(E)
    total_rows = queries.shape[0]
    poi_rows = pois.shape[0]
    width = math.gcd(total_rows, 1024)
    columns = jnp.arange(poi_rows, dtype=jnp.int32)
    block_of = columns // TILE
    row_region = block_region[block_of]

    def one_block(carry, number):
        start = (number * width).astype(jnp.int32)
        query_rows = lax.dynamic_slice_in_dim(queries, start, width, 0)
        regions = lax.dynamic_slice_in_dim(query_region, start, width, 0)
        chosen = lax.dynamic_slice_in_dim(positive, start, width, 0)
        scores = jnp.dot(query_rows, pois.T, preferred_element_type=jnp.float32) * scale
        opened = (region_mask[regions][:, row_region] == 1) | (block_of[None, :] == (chosen // TILE)[:, None])
        masked = jnp.where(opened, scores, floor_value)
        highest = lax.optimization_barrier(jnp.max(masked, axis=1))
        total = lax.optimization_barrier(jnp.sum(jnp.where(opened, jnp.exp(scores - highest[:, None]), 0.0), axis=1))
        log_total = highest + jnp.log(total)
        is_pos = columns[None, :] == chosen[:, None]
        pos_score = lax.optimization_barrier(jnp.sum(jnp.where(is_pos, scores, 0.0), axis=1))
        losses = log_total - pos_score
        weights = (jnp.where(opened, jnp.exp(scores - log_total[:, None]), 0.0) - is_pos.astype(jnp.float32)).astype(jnp.bfloat16)
        query_part = jnp.dot(weights, pois, preferred_element_type=jnp.float32) * scale
        carry = carry + jnp.dot(weights.T, query_rows, preferred_element_type=jnp.float32)
        return (carry, (losses, query_part))
    start_grad = jnp.zeros((poi_rows, queries.shape[1]), jnp.float32)
    poi_sum, (losses, query_parts) = lax.scan(one_block, start_grad, jnp.arange(total_rows // width, dtype=jnp.int32))
    loss = losses.reshape(total_rows)
    query_grad = query_parts.reshape(total_rows, queries.shape[1])
    return (loss, query_grad, poi_sum * scale)
```

```python
import math

import jax
import jax.numpy as jnp
from jax import lax
from jax.experimental import pallas as pl
from jax.experimental.pallas import tpu as pltpu
from jax.sharding import PartitionSpec as P

MESH = pl.DeviceIdType.MESH
TILE = 128
EXT = 144
NX, NY, NZ = 4, 4, 8
PLANE = NX * NY
DZ = (0, 1, 7, 2, 6, 3, 5, 4)
MIRROR = tuple(DZ.index((NZ - d) % NZ) for d in DZ)
CLOSED = -1e30
FLOOR = -1e29
NT = (((1,), (1,)), ((), ()))
f32, bf16 = jnp.float32, jnp.bfloat16


def kernel(
    q_ref, p_ref, reg_ref, pos_ref, breg_ref, mask_ref,
    loss_ref, qg_ref, pg_ref,
    qall, pall, pt, hot, posf, bias, es, wts, mk, lk, ps, st, nrm, psr, acc,
    own, cbuf, crecv, zsend, zrecv, qsend, qrecv,
    q_ss, q_rs, p_ss, p_rs, f_ss, f_rs, n_ss, n_rs, s_ss, s_rs,
    c_ss, c_rs, z_ss, z_rs, g_ss, g_rs,
):
    blk = lax.axis_index("blk")
    dp = lax.axis_index("dp")
    core = blk % 2
    y = blk // 4
    x = dp % NX
    z = (dp // NX) * 2 + (blk // 2) % 2
    width = q_ref.shape[1]
    rows = q_ref.shape[0]
    nq = PLANE * rows
    scale = 1.0 / math.sqrt(width)

    def device(xx, yy, zz, cc):
        return (yy * 4 + (zz % 2) * 2 + cc, (zz // 2) * NX + xx)

    def plane_peer(dx, dy):
        return device((x + dx) % NX, (y + dy) % NY, z, core)

    def z_peer(dz):
        return device(x, y, (z + dz) % NZ, core)

    sibling = device(x, y, z, 1 - core)

    def remote(src, dst, ss, rs, dev):
        return pltpu.make_async_remote_copy(
            src_ref=src, dst_ref=dst, send_sem=ss, recv_sem=rs, device_id=dev, device_id_type=MESH
        )

    def back(slot):
        return ((NY - slot // NX) % NY) * NX + (NX - slot % NX) % NX

    barrier = pltpu.get_barrier_semaphore()
    for slot in range(1, PLANE):
        pl.semaphore_signal(barrier, inc=1, device_id=plane_peer(slot % NX, slot // NX), device_id_type=MESH)
    for dz in range(1, NZ):
        pl.semaphore_signal(barrier, inc=1, device_id=z_peer(dz), device_id_type=MESH)
    pl.semaphore_signal(barrier, inc=1, device_id=sibling, device_id_type=MESH)

    qall[0, :rows, :] = q_ref[...]
    pall[0, :rows, :] = p_ref[...]
    row = lax.broadcasted_iota(jnp.int32, (16, rows), 0)
    pos = pos_ref[...]
    small = jnp.where(row == 0, reg_ref[...], jnp.where(row == 1, pos // TILE, pos % TILE)).astype(f32)
    small = small.astype(bf16)
    qall[0, rows:, :rows] = small
    qall[0, rows:, rows:] = small
    pall[0, rows:, :] = jnp.full((16, width), breg_ref[0], jnp.int32).astype(f32).astype(bf16)

    pl.semaphore_wait(barrier, PLANE + NZ - 1)

    def q_copy(slot):
        return remote(qall.at[0], qall.at[back(slot)], q_ss.at[slot], q_rs.at[back(slot)],
                      plane_peer(slot % NX, slot // NX))

    def p_copy(t):
        return remote(pall.at[0], pall.at[2 * MIRROR[t]], p_ss.at[t], p_rs.at[MIRROR[t]], z_peer(DZ[t]))

    def f_copy(t):
        return remote(pall.at[2 * t], pall.at[2 * t + 1], f_ss.at[t], f_rs.at[t], sibling)

    f_copy(0).start()
    for t in range(1, NZ):
        p_copy(t).start()
    for slot in range(1, PLANE):
        q_copy(slot).start()

    ps[...] = jnp.zeros_like(ps)
    region_mask = mask_ref[...].astype(f32).astype(bf16)
    regions = region_mask.shape[0]

    def take_query_small(slot):
        extra = qall[slot, rows:, :rows].astype(f32)
        lanes = slice(slot * rows, (slot + 1) * rows)
        region_ids = lax.broadcasted_iota(jnp.int32, (regions, rows), 0).astype(f32)
        hot[:, lanes] = (region_ids == extra[0:1]).astype(f32).astype(bf16)
        posf[0:8, lanes] = jnp.broadcast_to(extra[1:2], (8, rows))
        posf[8:16, lanes] = jnp.broadcast_to(extra[2:3] + extra[1:2] * TILE, (8, rows))

    take_query_small(0)
    for slot in range(1, PLANE):
        q_copy(back(slot)).wait_recv()
        take_query_small(slot)

    lane64 = lax.broadcasted_iota(jnp.int32, (8, regions), 1).astype(f32)
    iota = lax.broadcasted_iota(jnp.int32, (rows, 256), 0).astype(f32)
    chunks = nq // 256
    log2e_scale = scale / math.log(2.0)

    def block_ids(t):
        zz = (z + DZ[t]) % NZ
        ids = []
        for cc in (core, 1 - core):
            b, d = device(x, y, zz, cc)
            ids.append((b * 16 + d).astype(f32))
        return ids

    def group_sum(v):
        return jnp.sum(v.reshape(v.shape[0] // 8, 8, v.shape[1]), axis=0)

    for t in range(NZ):
        if t > 0:
            p_copy(MIRROR[t]).wait_recv()
            f_copy(t).start()
        f_copy(t).wait_recv()
        ids = block_ids(t)
        hots = [
            (lane64 == pall[2 * t + h, rows:rows + 8, :regions].astype(f32)).astype(f32)
            for h in range(2)
        ]
        picked = lax.dot_general(
            jnp.concatenate(hots, axis=0).astype(bf16), region_mask, NT, preferred_element_type=f32
        ).astype(bf16)
        opened = jnp.dot(picked, hot[...], preferred_element_type=f32)
        for h in range(2):
            part = (opened[8 * h:8 * h + 8] > 0.5) | (posf[0:8, :] == ids[h])
            bias[8 * h:8 * h + 8, :] = jnp.where(part, 0.0, CLOSED)
        pt[:, t * 256:(t + 1) * 256] = pall[2 * t:2 * t + 2, :rows, :].reshape(256, width).T

        def score_chunk(g, carry, t=t, ids=ids):
            lanes = pl.ds(pl.multiple_of(g * 256, 256), 256)
            pair = pall[2 * t:2 * t + 2, :rows, :].reshape(256, width)
            qg = qall[pl.ds(2 * g, 2), :rows, :].reshape(256, width)
            s = lax.dot_general(pair, qg, NT, preferred_element_type=f32)
            target = posf[8:9, lanes]
            high = None
            found = ps[:, lanes]
            shifted = []
            for h in range(2):
                part = s[h * rows:(h + 1) * rows]
                found += group_sum(jnp.where(iota == target - ids[h] * TILE, part, 0.0))
                part = part.reshape(16, 8, 256) * log2e_scale + bias[8 * h:8 * h + 8, lanes][None]
                shifted.append(part)
                top = jnp.max(part, axis=0)
                high = top if high is None else jnp.maximum(high, top)
            ps[:, lanes] = found
            high = jnp.maximum(jnp.max(high, axis=0, keepdims=True), FLOOR)
            high = jnp.broadcast_to(high, (8, 256))
            mk[t, :, lanes] = high
            total = jnp.zeros((8, 256), f32)
            for h in range(2):
                e = jnp.exp2(shifted[h] - high[None])
                total += jnp.sum(e, axis=0)
                es[t, h * rows:(h + 1) * rows, lanes] = e.reshape(rows, 256)
            lk[t, :, lanes] = total
            return carry

        lax.fori_loop(0, chunks, score_chunk, 0)

    high = mk[0]
    for t in range(1, NZ):
        high = jnp.maximum(high, mk[t])
    total = jnp.zeros((8, nq), f32)
    for t in range(NZ):
        total += lk[t] * jnp.exp2(mk[t] - high)
    st[0:1, :] = high[0:1]
    st[1:2, :] = jnp.sum(total, axis=0, keepdims=True)

    def n_copy(slot):
        return remote(st, nrm.at[back(slot)], n_ss.at[slot], n_rs.at[back(slot)],
                      plane_peer(slot % NX, slot // NX))

    def s_copy(slot):
        return remote(ps.at[:, slot * rows:(slot + 1) * rows], psr.at[back(slot)], s_ss.at[slot],
                      s_rs.at[back(slot)], plane_peer(slot % NX, slot // NX))

    for slot in range(1, PLANE):
        n_copy(slot).start()
    for slot in range(1, PLANE):
        s_copy(slot).start()

    parts = [st[...]]
    for slot in range(1, PLANE):
        n_copy(back(slot)).wait_recv()
        sx, sy = slot % NX, slot // NX
        pieces = []
        for mine in range(PLANE):
            theirs = ((mine // NX - sy) % NY) * NX + (mine % NX - sx) % NX
            pieces.append(nrm[slot, :, theirs * rows:(theirs + 1) * rows])
        parts.append(jnp.concatenate(pieces, axis=1))
    high = parts[0][0:1]
    for part in parts[1:]:
        high = jnp.maximum(high, part[0:1])
    total = jnp.zeros((1, nq), f32)
    for part in parts:
        total += part[1:2] * jnp.exp2(part[0:1] - high)
    log_total = high + jnp.log2(total)
    for t in range(NZ):
        mk[t] = jnp.exp2(mk[t] - log_total)
    lsum = log_total[:, :rows] * math.log(2.0)

    def c_copy(t):
        return remote(cbuf.at[t], crecv.at[t], c_ss.at[t], c_rs.at[t], sibling)

    def z_copy(t):
        return remote(zsend.at[t], zrecv.at[MIRROR[t]], z_ss.at[t], z_rs.at[MIRROR[t]], z_peer(DZ[t]))

    def combine(t):
        c_copy(t).wait_recv()
        zsend[t] = own[t] + crecv[t]
        if t > 0:
            z_copy(t).start()

    order = tuple(range(NZ - 1, -1, -1))
    for number, t in enumerate(order):
        ids = block_ids(t)

        acc[...] = jnp.zeros_like(acc)

        def weight_chunk(g, carry, t=t, ids=ids):
            lanes = pl.ds(pl.multiple_of(g * 256, 256), 256)
            target = posf[8:9, lanes]
            factor = mk[t, :, lanes]
            halves = []
            for h in range(2):
                e = es[t, h * rows:(h + 1) * rows, lanes].reshape(16, 8, 256) * factor[None]
                e = e.reshape(rows, 256)
                halves.append(jnp.where(iota == target - ids[h] * TILE, e - 1.0, e).astype(bf16))
            w = jnp.concatenate(halves, axis=0)
            wts[t * 256:(t + 1) * 256, lanes] = w
            qg = qall[pl.ds(2 * g, 2), :rows, :].reshape(256, width)
            acc[...] += jnp.dot(w, qg, preferred_element_type=f32)
            return carry

        lax.fori_loop(0, chunks, weight_chunk, 0)
        own[t] = acc[:rows]
        cbuf[t] = acc[rows:]
        c_copy(t).start()
        if number > 0:
            combine(order[number - 1])
    combine(order[-1])

    def g_copy(slot):
        return remote(qsend.at[slot], qrecv.at[back(slot)], g_ss.at[slot], g_rs.at[back(slot)],
                      plane_peer(slot % NX, slot // NX))

    def query_chunk(g):
        lanes = pl.ds(pl.multiple_of(g * 256, 256), 256)
        grad = jnp.dot(pt[...], wts[:, lanes], preferred_element_type=f32)
        qsend[2 * g] = grad[:, :rows]
        qsend[2 * g + 1] = grad[:, rows:]

    def query_step(g, carry):
        query_chunk(g)
        g_copy(2 * g).start()
        g_copy(2 * g + 1).start()
        return carry

    lax.fori_loop(1, chunks, query_step, 0)
    query_chunk(0)
    g_copy(1).start()

    found = ps[:, :rows]
    for slot in range(1, PLANE):
        s_copy(back(slot)).wait_recv()
        found += psr[slot]
    loss_ref[...] = lsum - jnp.sum(found, axis=0, keepdims=True) * scale

    grads = zsend[0]
    for t in range(1, NZ):
        z_copy(MIRROR[t]).wait_recv()
        grads += zrecv[t]
    pg_ref[...] = grads * scale

    grads = qsend[0]
    for slot in range(1, PLANE):
        g_copy(back(slot)).wait_recv()
        grads += qrecv[slot]
    qg_ref[...] = (grads * scale).T

    for t in range(NZ):
        f_copy(t).wait_send()
        c_copy(t).wait_send()
    for t in range(1, NZ):
        p_copy(t).wait_send()
        z_copy(t).wait_send()
    for slot in range(1, PLANE):
        q_copy(slot).wait_send()
        n_copy(slot).wait_send()
        s_copy(slot).wait_send()
        g_copy(slot).wait_send()


def body(queries, pois, query_region, block_region, region_mask, positive):
    rows, width = queries.shape
    regions = region_mask.shape[0]
    nq = PLANE * rows
    npoi = 2 * NZ * rows
    vmem = pl.BlockSpec(memory_space=pltpu.VMEM)
    dma = pltpu.SemaphoreType.DMA
    loss, query_grad, poi_grad = pl.pallas_call(
        kernel,
        out_shape=(
            jax.ShapeDtypeStruct((1, rows), f32),
            jax.ShapeDtypeStruct((rows, width), f32),
            jax.ShapeDtypeStruct((rows, width), f32),
        ),
        in_specs=[vmem, vmem, vmem, vmem, pl.BlockSpec(memory_space=pltpu.SMEM), vmem],
        out_specs=(vmem, vmem, vmem),
        scratch_shapes=[
            pltpu.VMEM((PLANE, EXT, width), bf16),
            pltpu.VMEM((2 * NZ, EXT, width), bf16),
            pltpu.VMEM((width, npoi), bf16),
            pltpu.VMEM((regions, nq), bf16),
            pltpu.VMEM((16, nq), f32),
            pltpu.VMEM((16, nq), f32),
            pltpu.VMEM((NZ, 2 * rows, nq), f32),
            pltpu.VMEM((npoi, nq), bf16),
            pltpu.VMEM((NZ, 8, nq), f32),
            pltpu.VMEM((NZ, 8, nq), f32),
            pltpu.VMEM((8, nq), f32),
            pltpu.VMEM((2, nq), f32),
            pltpu.VMEM((PLANE, 2, nq), f32),
            pltpu.VMEM((PLANE, 8, rows), f32),
            pltpu.VMEM((2 * rows, width), f32),
            pltpu.VMEM((NZ, rows, width), f32),
            pltpu.VMEM((NZ, rows, width), f32),
            pltpu.VMEM((NZ, rows, width), f32),
            pltpu.VMEM((NZ, rows, width), f32),
            pltpu.VMEM((NZ, rows, width), f32),
            pltpu.VMEM((PLANE, width, rows), f32),
            pltpu.VMEM((PLANE, width, rows), f32),
            dma((PLANE,)), dma((PLANE,)), dma((NZ,)), dma((NZ,)), dma((NZ,)), dma((NZ,)),
            dma((PLANE,)), dma((PLANE,)), dma((PLANE,)), dma((PLANE,)),
            dma((NZ,)), dma((NZ,)), dma((NZ,)), dma((NZ,)), dma((PLANE,)), dma((PLANE,)),
        ],
        compiler_params=pltpu.CompilerParams(
            collective_id=0, has_side_effects=True, vmem_limit_bytes=56 * 2**20
        ),
    )(
        queries, pois, query_region.reshape(1, rows), positive.reshape(1, rows), block_region, region_mask
    )
    return (loss.reshape(rows), query_grad, poi_grad)


def solution(mesh):
    in_specs = (
        P(("blk", "dp"), None),
        P(("blk", "dp"), None),
        P(("blk", "dp")),
        P(("blk", "dp")),
        P(),
        P(("blk", "dp")),
    )
    out_specs = (P(("blk", "dp")), P(("blk", "dp"), None), P(("blk", "dp"), None))
    return jax.shard_map(body, mesh=mesh, in_specs=in_specs, out_specs=out_specs, check_vma=False)
```

```python
import math

import jax
import jax.numpy as jnp
from jax import lax
from jax.experimental import pallas as pl
from jax.experimental.pallas import tpu as pltpu
from jax.sharding import PartitionSpec as P

MESH = pl.DeviceIdType.MESH
TILE = 128
EXT = 144
NX, NY, NZ = 4, 4, 8
PLANE = NX * NY
DZ = (0, 1, 7, 2, 6, 3, 5, 4)
ZBACK = tuple(DZ.index((NZ - d) % NZ) for d in DZ)
DXY = (
    (0, 0), (1, 0), (3, 0), (0, 1), (0, 3), (1, 1), (3, 3), (1, 3),
    (3, 1), (2, 0), (0, 2), (2, 1), (2, 3), (1, 2), (3, 2), (2, 2),
)
BACK = tuple(DXY.index(((NX - a) % NX, (NY - b) % NY)) for a, b in DXY)
CLOSED = -1e30
FLOOR = -1e29
TOP = 32767.0
NT = (((1,), (1,)), ((), ()))
f32, bf16 = jnp.float32, jnp.bfloat16


def quantized(v):
    top = jnp.max(jnp.abs(v.reshape(v.shape[0] // 8, 8, v.shape[1])), axis=0)
    top = jnp.max(top, axis=0, keepdims=True)
    step = jnp.where(top > 0.0, TOP / top, 0.0)
    return jnp.round(v * step).astype(jnp.int32).astype(jnp.int16), top * (1.0 / TOP)


def kernel(
    q_ref, p_ref, reg_ref, pos_ref, breg_ref, mask_ref,
    loss_ref, qg_ref, pg_ref,
    qall, pall, pt, hot, pick, tg, bias, es, wts, mk, lk, ps, st, nrm, side, sidr,
    own, cbuf, crecv, zown, zsend, zrecv, zstep, zstepr, qown, qsend, qrecv,
    q_ss, q_rs, p_ss, p_rs, f_ss, f_rs, n_ss, n_rs, s_ss, s_rs,
    c_ss, c_rs, z_ss, z_rs, y_ss, y_rs, g_ss, g_rs,
):
    blk = lax.axis_index("blk")
    dp = lax.axis_index("dp")
    core = blk % 2
    y = blk // 4
    x = dp % NX
    z = (dp // NX) * 2 + (blk // 2) % 2
    width = q_ref.shape[1]
    rows = q_ref.shape[0]
    nq = PLANE * rows
    scale = 1.0 / math.sqrt(width)

    def device(xx, yy, zz, cc):
        return (yy * 4 + (zz % 2) * 2 + cc, (zz // 2) * NX + xx)

    def plane_peer(slot):
        return device((x + DXY[slot][0]) % NX, (y + DXY[slot][1]) % NY, z, core)

    def z_peer(t):
        return device(x, y, (z + DZ[t]) % NZ, core)

    sibling = device(x, y, z, 1 - core)

    def remote(src, dst, ss, rs, dev):
        return pltpu.make_async_remote_copy(
            src_ref=src, dst_ref=dst, send_sem=ss, recv_sem=rs, device_id=dev, device_id_type=MESH
        )

    barrier = pltpu.get_barrier_semaphore()
    for slot in range(1, PLANE):
        pl.semaphore_signal(barrier, inc=1, device_id=plane_peer(slot), device_id_type=MESH)
    for t in range(1, NZ):
        pl.semaphore_signal(barrier, inc=1, device_id=z_peer(t), device_id_type=MESH)
    pl.semaphore_signal(barrier, inc=1, device_id=sibling, device_id_type=MESH)

    qall[0, :rows, :] = q_ref[...]
    pall[0, :rows, :] = p_ref[...]
    row = lax.broadcasted_iota(jnp.int32, (16, rows), 0)
    pos = pos_ref[...]
    small = jnp.where(row == 0, reg_ref[...], jnp.where(row == 1, pos // TILE, pos % TILE)).astype(f32)
    small = small.astype(bf16)
    qall[0, rows:, :rows] = small
    qall[0, rows:, rows:] = small
    pall[0, rows:, :] = jnp.full((16, width), breg_ref[0], jnp.int32).astype(f32).astype(bf16)

    pl.semaphore_wait(barrier, PLANE + NZ - 1)

    def q_copy(slot):
        return remote(qall.at[0], qall.at[BACK[slot]], q_ss.at[slot], q_rs.at[BACK[slot]], plane_peer(slot))

    def p_copy(t):
        return remote(pall.at[0], pall.at[2 * ZBACK[t]], p_ss.at[t], p_rs.at[ZBACK[t]], z_peer(t))

    def f_copy(t):
        return remote(pall.at[2 * t], pall.at[2 * t + 1], f_ss.at[t], f_rs.at[t], sibling)

    f_copy(0).start()
    for slot in range(1, PLANE):
        q_copy(slot).start()
        if slot < NZ:
            p_copy(slot).start()

    ps[...] = jnp.zeros_like(ps)
    region_mask = mask_ref[...].astype(f32).astype(bf16)
    regions = region_mask.shape[0]
    region_ids = lax.broadcasted_iota(jnp.int32, (regions, rows), 0).astype(f32)
    lane_ids = lax.broadcasted_iota(jnp.int32, (8, regions), 1).astype(f32)
    within = lax.broadcasted_iota(jnp.int32, (2 * rows, 256), 0) % rows
    within = within.astype(f32).reshape(2, 16, 8, 256)
    starts = []
    for t in range(NZ):
        for cc in (core, 1 - core):
            b, d = device(x, y, (z + DZ[t]) % NZ, cc)
            starts.append(((b * 16 + d) * TILE).astype(f32))

    def take_queries(slot):
        extra = qall[slot, rows:, :rows].astype(f32)
        lanes = slice(slot * rows, (slot + 1) * rows)
        hot[:, lanes] = (region_ids == extra[0:1]).astype(f32).astype(bf16)
        target = jnp.broadcast_to(extra[1:2] * TILE + extra[2:3], (8, rows))
        for k, start in enumerate(starts):
            tg[k // 2, 8 * (k % 2):8 * (k % 2) + 8, lanes] = target - start

    def take_pair(t):
        pair = pall[2 * t:2 * t + 2, :rows, :].reshape(256, width)
        pt[:, t * 256:(t + 1) * 256] = pair.T
        hots = [
            (lane_ids == pall[2 * t + h, rows:rows + 8, :regions].astype(f32)).astype(f32)
            for h in range(2)
        ]
        pick[16 * t:16 * t + 16, :] = lax.dot_general(
            jnp.concatenate(hots, axis=0).astype(bf16), region_mask, NT, preferred_element_type=f32
        ).astype(bf16)

    def set_bias(first, last, lanes):
        opened = jnp.dot(pick[16 * first:16 * last, :], hot[:, lanes], preferred_element_type=f32)
        for t in range(first, last):
            at = tg[t, :, lanes]
            part = (opened[16 * (t - first):16 * (t - first) + 16] > 0.5) | ((at >= 0.0) & (at < TILE))
            bias[t, :, lanes] = jnp.where(part, 0.0, CLOSED)

    log2e_scale = scale / math.log(2.0)

    def score_tile(t, g):
        lanes = slice(g * 256, (g + 1) * 256)
        pair = pall[2 * t:2 * t + 2, :rows, :].reshape(256, width)
        qg = qall[2 * g:2 * g + 2, :rows, :].reshape(256, width)
        s = lax.dot_general(pair, qg, NT, preferred_element_type=f32).reshape(2, 16, 8, 256)
        target = tg[t, :, lanes].reshape(2, 1, 8, 256)
        ps[:, lanes] += jnp.sum(jnp.where(within == target, s, 0.0), axis=(0, 1))
        s = s * log2e_scale + bias[t, :, lanes].reshape(2, 1, 8, 256)
        high = jnp.max(jnp.max(s, axis=(0, 1)), axis=0, keepdims=True)
        high = jnp.broadcast_to(jnp.maximum(high, FLOOR), (8, 256))
        mk[t, :, lanes] = high
        e = jnp.exp2(s - high)
        lk[t, :, lanes] = jnp.sum(e, axis=(0, 1))
        es[t, :, lanes] = e.reshape(256, 256)

    chunks = nq // 256
    for k in range(NZ):
        for slot in (2 * k, 2 * k + 1):
            if slot > 0:
                q_copy(BACK[slot]).wait_recv()
        if k > 0:
            p_copy(ZBACK[k]).wait_recv()
            f_copy(k).start()
        take_queries(2 * k)
        take_queries(2 * k + 1)
        f_copy(k).wait_recv()
        take_pair(k)
        set_bias(0, k + 1, slice(k * 256, (k + 1) * 256))
        if k > 0:
            set_bias(k, k + 1, slice(0, k * 256))
        for t in range(k):
            score_tile(t, k)
        for g in range(k + 1):
            score_tile(k, g)

    high = mk[0]
    for t in range(1, NZ):
        high = jnp.maximum(high, mk[t])
    total = jnp.zeros((8, nq), f32)
    for t in range(NZ):
        total += lk[t] * jnp.exp2(mk[t] - high)
    total = jnp.sum(total, axis=0, keepdims=True)
    st[...] = jnp.where(total > 0.0, high[0:1] + jnp.log2(jnp.where(total > 0.0, total, 1.0)), CLOSED)

    def n_copy(slot):
        return remote(st, nrm.at[BACK[slot]], n_ss.at[slot], n_rs.at[BACK[slot]], plane_peer(slot))

    for slot in range(PLANE - 1, 0, -1):
        n_copy(slot).start()
    parts = [st[...]]
    for slot in range(1, PLANE):
        n_copy(BACK[slot]).wait_recv()
        pieces = []
        for a, b in DXY:
            theirs = DXY.index(((a - DXY[slot][0]) % NX, (b - DXY[slot][1]) % NY))
            pieces.append(nrm[slot, :, theirs * rows:(theirs + 1) * rows])
        parts.append(jnp.concatenate(pieces, axis=1))
    high = parts[0]
    for part in parts[1:]:
        high = jnp.maximum(high, part)
    total = jnp.zeros((1, nq), f32)
    for part in parts:
        total += jnp.exp2(part - high)
    log_total = high + jnp.log2(total)
    for t in range(NZ):
        mk[t] = jnp.exp2(mk[t] - log_total)
    lsum = log_total[:, :rows] * math.log(2.0)

    def c_copy(t):
        return remote(cbuf.at[t], crecv.at[t], c_ss.at[t], c_rs.at[t], sibling)

    def z_copy(t):
        return remote(zsend.at[t], zrecv.at[ZBACK[t]], z_ss.at[t], z_rs.at[ZBACK[t]], z_peer(t))

    def y_copy(t):
        return remote(zstep.at[t], zstepr.at[ZBACK[t]], y_ss.at[t], y_rs.at[ZBACK[t]], z_peer(t))

    def combine(t):
        c_copy(t).wait_recv()
        both = own[t] + crecv[t]
        if t == 0:
            zown[...] = both
        else:
            zsend[t], zstep[t] = quantized(both)
            z_copy(t).start()
            y_copy(t).start()

    order = tuple(range(NZ - 1, -1, -1))
    for number, t in enumerate(order):
        for g in range(chunks):
            lanes = slice(g * 256, (g + 1) * 256)
            e = es[t, :, lanes].reshape(2, 16, 8, 256) * mk[t, :, lanes]
            target = tg[t, :, lanes].reshape(2, 1, 8, 256)
            w = jnp.where(within == target, e - 1.0, e).reshape(256, 256).astype(bf16)
            wts[t * 256:(t + 1) * 256, lanes] = w
        grad = jnp.zeros((256, width), f32)
        for g in range(chunks):
            grad += jnp.dot(
                wts[t * 256:(t + 1) * 256, g * 256:(g + 1) * 256],
                qall[2 * g:2 * g + 2, :rows, :].reshape(256, width),
                preferred_element_type=f32,
            )
        own[t] = grad[:rows]
        cbuf[t] = grad[rows:]
        c_copy(t).start()
        if number > 0:
            combine(order[number - 1])
    combine(order[-1])

    def g_copy(slot):
        return remote(qsend.at[slot], qrecv.at[BACK[slot]], g_ss.at[slot], g_rs.at[BACK[slot]], plane_peer(slot))

    def s_copy(slot):
        return remote(side.at[slot], sidr.at[BACK[slot]], s_ss.at[slot], s_rs.at[BACK[slot]], plane_peer(slot))

    eight = lax.broadcasted_iota(jnp.int32, (8, rows), 0)
    for g in range(chunks - 1, -1, -1):
        grad = jnp.dot(pt[...], wts[:, g * 256:(g + 1) * 256], preferred_element_type=f32)
        for half in range(2):
            slot = 2 * g + half
            piece = grad[:, half * rows:(half + 1) * rows]
            if slot == 0:
                qown[...] = piece
            else:
                qsend[slot], step = quantized(piece)
                found = jnp.sum(ps[:, slot * rows:(slot + 1) * rows], axis=0, keepdims=True)
                side[slot] = jnp.where(eight == 0, found, step)
                g_copy(slot).start()
                s_copy(slot).start()

    grads = zown[...]
    for t in range(1, NZ):
        z_copy(ZBACK[t]).wait_recv()
        y_copy(ZBACK[t]).wait_recv()
        grads += zrecv[t].astype(jnp.int32).astype(f32) * zstepr[t]
    pg_ref[...] = grads * scale

    found = jnp.sum(ps[:, :rows], axis=0, keepdims=True)
    grads = qown[...]
    for slot in range(PLANE - 1, 0, -1):
        g_copy(BACK[slot]).wait_recv()
        s_copy(BACK[slot]).wait_recv()
        found += sidr[slot, 0:1]
        grads += qrecv[slot].astype(jnp.int32).astype(f32) * sidr[slot, 1:2]
    loss_ref[...] = lsum - found * scale
    qg_ref[...] = (grads * scale).T

    for t in range(NZ):
        f_copy(t).wait_send()
        c_copy(t).wait_send()
    for t in range(1, NZ):
        p_copy(t).wait_send()
        z_copy(t).wait_send()
        y_copy(t).wait_send()
    for slot in range(1, PLANE):
        q_copy(slot).wait_send()
        n_copy(slot).wait_send()
        s_copy(slot).wait_send()
        g_copy(slot).wait_send()


def body(queries, pois, query_region, block_region, region_mask, positive):
    rows, width = queries.shape
    regions = region_mask.shape[0]
    nq = PLANE * rows
    npoi = 2 * NZ * rows
    vmem = pl.BlockSpec(memory_space=pltpu.VMEM)
    dma = pltpu.SemaphoreType.DMA
    loss, query_grad, poi_grad = pl.pallas_call(
        kernel,
        out_shape=(
            jax.ShapeDtypeStruct((1, rows), f32),
            jax.ShapeDtypeStruct((rows, width), f32),
            jax.ShapeDtypeStruct((rows, width), f32),
        ),
        in_specs=[vmem, vmem, vmem, vmem, pl.BlockSpec(memory_space=pltpu.SMEM), vmem],
        out_specs=(vmem, vmem, vmem),
        scratch_shapes=[
            pltpu.VMEM((PLANE, EXT, width), bf16),
            pltpu.VMEM((2 * NZ, EXT, width), bf16),
            pltpu.VMEM((width, npoi), bf16),
            pltpu.VMEM((regions, nq), bf16),
            pltpu.VMEM((16 * NZ, regions), bf16),
            pltpu.VMEM((NZ, 16, nq), f32),
            pltpu.VMEM((NZ, 16, nq), f32),
            pltpu.VMEM((NZ, 2 * rows, nq), f32),
            pltpu.VMEM((npoi, nq), bf16),
            pltpu.VMEM((NZ, 8, nq), f32),
            pltpu.VMEM((NZ, 8, nq), f32),
            pltpu.VMEM((8, nq), f32),
            pltpu.VMEM((1, nq), f32),
            pltpu.VMEM((PLANE, 1, nq), f32),
            pltpu.VMEM((PLANE, 8, rows), f32),
            pltpu.VMEM((PLANE, 8, rows), f32),
            pltpu.VMEM((NZ, rows, width), f32),
            pltpu.VMEM((NZ, rows, width), f32),
            pltpu.VMEM((NZ, rows, width), f32),
            pltpu.VMEM((rows, width), f32),
            pltpu.VMEM((NZ, rows, width), jnp.int16),
            pltpu.VMEM((NZ, rows, width), jnp.int16),
            pltpu.VMEM((NZ, 1, width), f32),
            pltpu.VMEM((NZ, 1, width), f32),
            pltpu.VMEM((width, rows), f32),
            pltpu.VMEM((PLANE, width, rows), jnp.int16),
            pltpu.VMEM((PLANE, width, rows), jnp.int16),
            dma((PLANE,)), dma((PLANE,)), dma((NZ,)), dma((NZ,)), dma((NZ,)), dma((NZ,)),
            dma((PLANE,)), dma((PLANE,)), dma((PLANE,)), dma((PLANE,)),
            dma((NZ,)), dma((NZ,)), dma((NZ,)), dma((NZ,)), dma((NZ,)), dma((NZ,)),
            dma((PLANE,)), dma((PLANE,)),
        ],
        compiler_params=pltpu.CompilerParams(
            collective_id=0, has_side_effects=True, vmem_limit_bytes=56 * 2**20
        ),
    )(
        queries, pois, query_region.reshape(1, rows), positive.reshape(1, rows), block_region, region_mask
    )
    return (loss.reshape(rows), query_grad, poi_grad)


def solution(mesh):
    in_specs = (
        P(("blk", "dp"), None),
        P(("blk", "dp"), None),
        P(("blk", "dp")),
        P(("blk", "dp")),
        P(),
        P(("blk", "dp")),
    )
    out_specs = (P(("blk", "dp")), P(("blk", "dp"), None), P(("blk", "dp"), None))
    return jax.shard_map(body, mesh=mesh, in_specs=in_specs, out_specs=out_specs, check_vma=False)
```

```python
import math

import jax
import jax.numpy as jnp
from jax import lax
from jax.experimental import pallas as pl
from jax.experimental.pallas import tpu as pltpu
from jax.sharding import PartitionSpec as P

MESH = pl.DeviceIdType.MESH
TILE = 128
EXT = 136
NX, NY, NZ = 4, 4, 8
PLANE = NX * NY
DZ = (0, 1, 7, 2, 6, 3, 5, 4)
ZBACK = tuple(DZ.index((NZ - d) % NZ) for d in DZ)
DXY = (
    (0, 0), (1, 0), (3, 0), (0, 1), (0, 3), (2, 0), (0, 2), (1, 1),
    (3, 3), (1, 3), (3, 1), (2, 1), (2, 3), (1, 2), (3, 2), (2, 2),
)
BACK = tuple(DXY.index(((NX - a) % NX, (NY - b) % NY)) for a, b in DXY)
AXIS = 7
HALF = 64
LAG = 8
CLOSED = -1e30
FLOOR = -1e29
TOP = 32767.0
NT = (((1,), (1,)), ((), ()))
f32, bf16 = jnp.float32, jnp.bfloat16


def quantized(v):
    top = jnp.max(jnp.abs(v.reshape(v.shape[0] // 8, 8, v.shape[1])), axis=0)
    top = jnp.max(top, axis=0, keepdims=True)
    step = jnp.where(top > 0.0, TOP / top, 0.0)
    return jnp.round(v * step).astype(jnp.int32).astype(jnp.int16), top * (1.0 / TOP)


def kernel(
    q_ref, p_ref, reg_ref, pos_ref, breg_ref, mask_ref,
    loss_ref, qg_ref, pg_ref,
    qall, pall, pt, hot, pick, tg, bias, es, wts, mk, lk, ps, st, nrm, side, sidr,
    own, cbuf, crecv, zown, zsend, zrecv, zstep, zstepr, qown, qsend, qrecv,
    q_ss, q_rs, h_ss, h_rs, p_ss, p_rs, f_ss, f_rs, n_ss, n_rs, s_ss, s_rs,
    c_ss, c_rs, z_ss, z_rs, y_ss, y_rs, g_ss, g_rs,
):
    blk = lax.axis_index("blk")
    dp = lax.axis_index("dp")
    core = blk % 2
    y = blk // 4
    x = dp % NX
    z = (dp // NX) * 2 + (blk // 2) % 2
    width = q_ref.shape[1]
    rows = q_ref.shape[0]
    nq = PLANE * rows
    scale = 1.0 / math.sqrt(width)

    def device(xx, yy, zz, cc):
        return (yy * 4 + (zz % 2) * 2 + cc, (zz // 2) * NX + xx)

    def plane_peer(slot):
        return device((x + DXY[slot][0]) % NX, (y + DXY[slot][1]) % NY, z, core)

    def z_peer(t):
        return device(x, y, (z + DZ[t]) % NZ, core)

    sibling = device(x, y, z, 1 - core)

    def remote(src, dst, ss, rs, dev):
        return pltpu.make_async_remote_copy(
            src_ref=src, dst_ref=dst, send_sem=ss, recv_sem=rs, device_id=dev, device_id_type=MESH
        )

    barrier = pltpu.get_barrier_semaphore()
    for slot in range(1, PLANE):
        pl.semaphore_signal(barrier, inc=1, device_id=plane_peer(slot), device_id_type=MESH)
    for t in range(1, NZ):
        pl.semaphore_signal(barrier, inc=1, device_id=z_peer(t), device_id_type=MESH)
    pl.semaphore_signal(barrier, inc=1, device_id=sibling, device_id_type=MESH)

    qall[0, :rows, :] = q_ref[...]
    pall[0, :rows, :] = p_ref[...]
    row = lax.broadcasted_iota(jnp.int32, (EXT - rows, rows), 0)
    pos = pos_ref[...]
    small = jnp.where(row == 0, reg_ref[...], jnp.where(row == 1, pos // TILE, pos % TILE)).astype(f32)
    small = small.astype(bf16)
    qall[0, rows:, :rows] = small
    qall[0, rows:, rows:] = small
    pall[0, rows:, :] = jnp.full((EXT - rows, width), breg_ref[0], jnp.int32).astype(f32).astype(bf16)

    pl.semaphore_wait(barrier, PLANE + NZ - 1)

    def q_copy(slot):
        return remote(qall.at[0], qall.at[BACK[slot]], q_ss.at[slot], q_rs.at[BACK[slot]], plane_peer(slot))

    def h_copy(slot, peer):
        a, b = DXY[slot]
        c, d = DXY[peer]
        there = DXY.index(((a - c) % NX, (b - d) % NY))
        part = slice(0, HALF) if b == 0 else slice(HALF, EXT)
        k = 2 * there + (0 if b == 0 else 1)
        return remote(qall.at[slot, part], qall.at[there, part], h_ss.at[k], h_rs.at[k], plane_peer(peer))

    def pass_on(slot):
        a, b = DXY[slot]
        return [h_copy(slot, DXY.index((0, d) if b == 0 else (d, 0))) for d in (1, 3, 2)]

    def p_copy(slot, part, t, k, dz):
        return remote(pall.at[2 * slot, part], pall.at[2 * t, part], p_ss.at[k], p_rs.at[k], z_peer(DZ.index(dz)))

    def p_next(t):
        whole, low, high = slice(0, EXT), slice(0, HALF), slice(HALF, EXT)
        if t == 0:
            return [p_copy(0, whole, ZBACK[k], ZBACK[k], DZ[k]) for k in (3, 4, 1, 2)]
        if DZ[t] == 2:
            return [p_copy(t, low, 7, 7, NZ - 2), p_copy(t, whole, 5, 5, NZ - 1)]
        if DZ[t] == 6:
            return [p_copy(t, high, 7, 8, 2), p_copy(t, whole, 6, 6, 1)]
        return []

    def p_wait(t):
        if t < 7:
            p_copy(0, slice(0, EXT), t, t, 1).wait_recv()
        else:
            p_copy(0, slice(0, HALF), 7, 7, 1).wait_recv()
            p_copy(0, slice(HALF, EXT), 7, 8, 1).wait_recv()

    def f_copy(t):
        return remote(pall.at[2 * t], pall.at[2 * t + 1], f_ss.at[t], f_rs.at[t], sibling)

    for copy in p_next(0):
        copy.start()
    for slot in range(1, AXIS):
        q_copy(slot).start()
    f_copy(0).start()

    ps[...] = jnp.zeros_like(ps)
    region_mask = mask_ref[...].astype(f32).astype(bf16)
    regions = region_mask.shape[0]
    region_ids = lax.broadcasted_iota(jnp.int32, (regions, rows), 0).astype(f32)
    lane_ids = lax.broadcasted_iota(jnp.int32, (8, regions), 1).astype(f32)
    within = lax.broadcasted_iota(jnp.int32, (2 * rows, 256), 0) % rows
    within = within.astype(f32).reshape(2, 16, 8, 256)
    starts = []
    for t in range(NZ):
        for cc in (core, 1 - core):
            b, d = device(x, y, (z + DZ[t]) % NZ, cc)
            starts.append(((b * 16 + d) * TILE).astype(f32))

    def take_queries(slot):
        extra = qall[slot, rows:, :rows].astype(f32)
        lanes = slice(slot * rows, (slot + 1) * rows)
        hot[:, lanes] = (region_ids == extra[0:1]).astype(f32).astype(bf16)
        target = jnp.broadcast_to(extra[1:2] * TILE + extra[2:3], (8, rows))
        for k, start in enumerate(starts):
            tg[k // 2, 8 * (k % 2):8 * (k % 2) + 8, lanes] = target - start

    def take_pair(t):
        pair = pall[2 * t:2 * t + 2, :rows, :].reshape(256, width)
        pt[:, t * 256:(t + 1) * 256] = pair.T
        hots = [
            (lane_ids == pall[2 * t + h, rows:rows + 8, :regions].astype(f32)).astype(f32)
            for h in range(2)
        ]
        pick[16 * t:16 * t + 16, :] = lax.dot_general(
            jnp.concatenate(hots, axis=0).astype(bf16), region_mask, NT, preferred_element_type=f32
        ).astype(bf16)

    def set_bias(first, last, lanes):
        opened = jnp.dot(pick[16 * first:16 * last, :], hot[:, lanes], preferred_element_type=f32)
        for t in range(first, last):
            at = tg[t, :, lanes]
            part = (opened[16 * (t - first):16 * (t - first) + 16] > 0.5) | ((at >= 0.0) & (at < TILE))
            bias[t, :, lanes] = jnp.where(part, 0.0, CLOSED)

    log2e_scale = scale / math.log(2.0)

    def score_tile(t, g):
        lanes = slice(g * 256, (g + 1) * 256)
        pair = pall[2 * t:2 * t + 2, :rows, :].reshape(256, width)
        qg = qall[2 * g:2 * g + 2, :rows, :].reshape(256, width)
        s = lax.dot_general(pair, qg, NT, preferred_element_type=f32).reshape(2, 16, 8, 256)
        target = tg[t, :, lanes].reshape(2, 1, 8, 256)
        ps[:, lanes] += jnp.sum(jnp.where(within == target, s, 0.0), axis=(0, 1))
        s = s * log2e_scale + bias[t, :, lanes].reshape(2, 1, 8, 256)
        high = jnp.max(jnp.max(s, axis=(0, 1)), axis=0, keepdims=True)
        high = jnp.broadcast_to(jnp.maximum(high, FLOOR), (8, 256))
        mk[t, :, lanes] = high
        e = jnp.exp2(s - high)
        lk[t, :, lanes] = jnp.sum(e, axis=(0, 1))
        es[t, :, lanes] = e.reshape(256, 256)

    chunks = nq // 256
    ready = {"t": 0, "g": 0}

    def arrived_queries(slot):
        if slot > 0:
            q_copy(BACK[slot]).wait_recv()
            for copy in pass_on(slot):
                copy.start()
        take_queries(slot)

    def arrived_shard(t):
        p_wait(t)
        for copy in p_next(t):
            copy.start()
        f_copy(t).start()

    def use_pair(t):
        f_copy(t).wait_recv()
        take_pair(t)
        ready["t"] = t + 1
        if ready["g"]:
            set_bias(t, t + 1, slice(0, ready["g"] * 256))
        for g in range(ready["g"]):
            score_tile(t, g)

    def use_chunk(g):
        for slot in (2 * g, 2 * g + 1):
            if slot >= AXIS:
                for half in range(2):
                    part = slice(0, HALF) if half == 0 else slice(HALF, EXT)
                    k = 2 * slot + half
                    remote(qall.at[slot, part], qall.at[slot, part], h_ss.at[k], h_rs.at[k], sibling).wait_recv()
                take_queries(slot)
        ready["g"] = g + 1
        if ready["t"]:
            set_bias(0, ready["t"], slice(g * 256, (g + 1) * 256))
        for t in range(ready["t"]):
            score_tile(t, g)

    steps = (
        (arrived_queries, (0, 1, 2, 3, 4)), (arrived_shard, (3, 4)), (arrived_queries, (5, 6)), (arrived_shard, (1, 2)),
        (use_pair, (0,)), (use_chunk, (0, 1, 2)), (use_pair, (1, 2, 3, 4)), (use_chunk, (3, 4)),
        (arrived_shard, (5, 6)), (use_chunk, (5,)), (arrived_shard, (7,)), (use_pair, (5, 6)), (use_chunk, (6, 7)),
        (use_pair, (7,)),
    )
    for step, items in steps:
        for item in items:
            step(item)

    high = mk[0]
    for t in range(1, NZ):
        high = jnp.maximum(high, mk[t])
    total = jnp.zeros((8, nq), f32)
    for t in range(NZ):
        total += lk[t] * jnp.exp2(mk[t] - high)
    total = jnp.sum(total, axis=0, keepdims=True)
    st[...] = jnp.where(total > 0.0, high[0:1] + jnp.log2(jnp.where(total > 0.0, total, 1.0)), CLOSED)

    def n_copy(slot):
        return remote(st, nrm.at[BACK[slot]], n_ss.at[slot], n_rs.at[BACK[slot]], plane_peer(slot))

    for slot in range(PLANE - 1, 0, -1):
        n_copy(slot).start()
    parts = [st[...]]
    for slot in range(1, PLANE):
        n_copy(BACK[slot]).wait_recv()
        pieces = []
        for a, b in DXY:
            theirs = DXY.index(((a - DXY[slot][0]) % NX, (b - DXY[slot][1]) % NY))
            pieces.append(nrm[slot, :, theirs * rows:(theirs + 1) * rows])
        parts.append(jnp.concatenate(pieces, axis=1))
    high = parts[0]
    for part in parts[1:]:
        high = jnp.maximum(high, part)
    total = jnp.zeros((1, nq), f32)
    for part in parts:
        total += jnp.exp2(part - high)
    log_total = high + jnp.log2(total)
    for t in range(NZ):
        mk[t] = jnp.exp2(mk[t] - log_total)
    lsum = log_total[:, :rows] * math.log(2.0)

    def c_copy(t):
        return remote(cbuf.at[t], crecv.at[t], c_ss.at[t], c_rs.at[t], sibling)

    def z_copy(t):
        return remote(zsend.at[t], zrecv.at[ZBACK[t]], z_ss.at[t], z_rs.at[ZBACK[t]], z_peer(t))

    def y_copy(t):
        return remote(zstep.at[t], zstepr.at[ZBACK[t]], y_ss.at[t], y_rs.at[ZBACK[t]], z_peer(t))

    def combine(t):
        c_copy(t).wait_recv()
        both = own[t] + crecv[t]
        if t == 0:
            zown[...] = both
        else:
            zsend[t], zstep[t] = quantized(both)
            z_copy(t).start()
            y_copy(t).start()

    order = tuple(range(NZ - 1, -1, -1))
    for number, t in enumerate(order):
        for g in range(chunks):
            lanes = slice(g * 256, (g + 1) * 256)
            e = es[t, :, lanes].reshape(2, 16, 8, 256) * mk[t, :, lanes]
            target = tg[t, :, lanes].reshape(2, 1, 8, 256)
            w = jnp.where(within == target, e - 1.0, e).reshape(256, 256).astype(bf16)
            wts[t * 256:(t + 1) * 256, lanes] = w
        grad = jnp.zeros((256, width), f32)
        for g in range(chunks):
            grad += jnp.dot(
                wts[t * 256:(t + 1) * 256, g * 256:(g + 1) * 256],
                qall[2 * g:2 * g + 2, :rows, :].reshape(256, width),
                preferred_element_type=f32,
            )
        own[t] = grad[:rows]
        cbuf[t] = grad[rows:]
        c_copy(t).start()
        if number >= LAG:
            combine(order[number - LAG])
    late = list(order[NZ - LAG:])

    def g_copy(slot):
        return remote(qsend.at[slot], qrecv.at[BACK[slot]], g_ss.at[slot], g_rs.at[BACK[slot]], plane_peer(slot))

    def s_copy(slot):
        return remote(side.at[slot], sidr.at[BACK[slot]], s_ss.at[slot], s_rs.at[BACK[slot]], plane_peer(slot))

    eight = lax.broadcasted_iota(jnp.int32, (8, rows), 0)
    for g in range(chunks - 1, -1, -1):
        grad = jnp.dot(pt[...], wts[:, g * 256:(g + 1) * 256], preferred_element_type=f32)
        for half in range(2):
            slot = 2 * g + half
            piece = grad[:, half * rows:(half + 1) * rows]
            if slot == 0:
                qown[...] = piece
            else:
                qsend[slot], step = quantized(piece)
                found = jnp.sum(ps[:, slot * rows:(slot + 1) * rows], axis=0, keepdims=True)
                side[slot] = jnp.where(eight == 0, found, step)
                g_copy(slot).start()
                s_copy(slot).start()
        combine(late.pop(0))

    grads = zown[...]
    for t in range(1, NZ):
        z_copy(ZBACK[t]).wait_recv()
        y_copy(ZBACK[t]).wait_recv()
        grads += zrecv[t].astype(jnp.int32).astype(f32) * zstepr[t]
    pg_ref[...] = grads * scale

    found = jnp.sum(ps[:, :rows], axis=0, keepdims=True)
    grads = qown[...]
    for slot in range(PLANE - 1, 0, -1):
        g_copy(BACK[slot]).wait_recv()
        s_copy(BACK[slot]).wait_recv()
        found += sidr[slot, 0:1]
        grads += qrecv[slot].astype(jnp.int32).astype(f32) * sidr[slot, 1:2]
    loss_ref[...] = lsum - found * scale
    qg_ref[...] = (grads * scale).T

    for t in range(NZ):
        f_copy(t).wait_send()
        c_copy(t).wait_send()
        for copy in p_next(t):
            copy.wait_send()
    for t in range(1, NZ):
        z_copy(t).wait_send()
        y_copy(t).wait_send()
    for slot in range(1, PLANE):
        n_copy(slot).wait_send()
        s_copy(slot).wait_send()
        g_copy(slot).wait_send()
    for slot in range(1, AXIS):
        q_copy(slot).wait_send()
        for copy in pass_on(slot):
            copy.wait_send()


def body(queries, pois, query_region, block_region, region_mask, positive):
    rows, width = queries.shape
    regions = region_mask.shape[0]
    nq = PLANE * rows
    npoi = 2 * NZ * rows
    vmem = pl.BlockSpec(memory_space=pltpu.VMEM)
    dma = pltpu.SemaphoreType.DMA
    loss, query_grad, poi_grad = pl.pallas_call(
        kernel,
        out_shape=(
            jax.ShapeDtypeStruct((1, rows), f32),
            jax.ShapeDtypeStruct((rows, width), f32),
            jax.ShapeDtypeStruct((rows, width), f32),
        ),
        in_specs=[vmem, vmem, vmem, vmem, pl.BlockSpec(memory_space=pltpu.SMEM), vmem],
        out_specs=(vmem, vmem, vmem),
        scratch_shapes=[
            pltpu.VMEM((PLANE, EXT, width), bf16),
            pltpu.VMEM((2 * NZ, EXT, width), bf16),
            pltpu.VMEM((width, npoi), bf16),
            pltpu.VMEM((regions, nq), bf16),
            pltpu.VMEM((16 * NZ, regions), bf16),
            pltpu.VMEM((NZ, 16, nq), f32),
            pltpu.VMEM((NZ, 16, nq), f32),
            pltpu.VMEM((NZ, 2 * rows, nq), f32),
            pltpu.VMEM((npoi, nq), bf16),
            pltpu.VMEM((NZ, 8, nq), f32),
            pltpu.VMEM((NZ, 8, nq), f32),
            pltpu.VMEM((8, nq), f32),
            pltpu.VMEM((1, nq), f32),
            pltpu.VMEM((PLANE, 1, nq), f32),
            pltpu.VMEM((PLANE, 8, rows), f32),
            pltpu.VMEM((PLANE, 8, rows), f32),
            pltpu.VMEM((NZ, rows, width), f32),
            pltpu.VMEM((NZ, rows, width), f32),
            pltpu.VMEM((NZ, rows, width), f32),
            pltpu.VMEM((rows, width), f32),
            pltpu.VMEM((NZ, rows, width), jnp.int16),
            pltpu.VMEM((NZ, rows, width), jnp.int16),
            pltpu.VMEM((NZ, 1, width), f32),
            pltpu.VMEM((NZ, 1, width), f32),
            pltpu.VMEM((width, rows), f32),
            pltpu.VMEM((PLANE, width, rows), jnp.int16),
            pltpu.VMEM((PLANE, width, rows), jnp.int16),
            dma((PLANE,)), dma((PLANE,)), dma((2 * PLANE,)), dma((2 * PLANE,)), dma((NZ + 1,)), dma((NZ + 1,)),
            dma((NZ,)), dma((NZ,)), dma((PLANE,)), dma((PLANE,)), dma((PLANE,)), dma((PLANE,)),
            dma((NZ,)), dma((NZ,)), dma((NZ,)), dma((NZ,)), dma((NZ,)), dma((NZ,)),
            dma((PLANE,)), dma((PLANE,)),
        ],
        compiler_params=pltpu.CompilerParams(
            collective_id=0, has_side_effects=True, vmem_limit_bytes=56 * 2**20
        ),
    )(
        queries, pois, query_region.reshape(1, rows), positive.reshape(1, rows), block_region, region_mask
    )
    return (loss.reshape(rows), query_grad, poi_grad)


def solution(mesh):
    in_specs = (
        P(("blk", "dp"), None),
        P(("blk", "dp"), None),
        P(("blk", "dp")),
        P(("blk", "dp")),
        P(),
        P(("blk", "dp")),
    )
    out_specs = (P(("blk", "dp")), P(("blk", "dp"), None), P(("blk", "dp"), None))
    return jax.shard_map(body, mesh=mesh, in_specs=in_specs, out_specs=out_specs, check_vma=False)
```

```python
import math

import jax
import jax.numpy as jnp
from jax import lax
from jax.experimental import pallas as pl
from jax.experimental.pallas import tpu as pltpu
from jax.sharding import PartitionSpec as P

MESH = pl.DeviceIdType.MESH
TILE = 128
EXT = 136
NX, NY, NZ = 4, 4, 8
PLANE = NX * NY
DZ = (0, 1, 7, 2, 6, 3, 5, 4)
ZBACK = tuple(DZ.index((NZ - d) % NZ) for d in DZ)
DXY = (
    (0, 0), (1, 0), (3, 0), (0, 1), (0, 3), (2, 0), (0, 2), (1, 1),
    (3, 3), (1, 3), (3, 1), (2, 1), (2, 3), (1, 2), (3, 2), (2, 2),
)
BACK = tuple(DXY.index(((NX - a) % NX, (NY - b) % NY)) for a, b in DXY)
AXIS = 7
HALF = 64
LAG = 2
CLOSED = -1e30
FLOOR = -1e29
TOP = 32767.0
NT = (((1,), (1,)), ((), ()))
f32, bf16 = jnp.float32, jnp.bfloat16


def quantized(v):
    top = jnp.max(jnp.abs(v.reshape(v.shape[0] // 8, 8, v.shape[1])), axis=0)
    top = jnp.max(top, axis=0, keepdims=True)
    step = jnp.where(top > 0.0, TOP / top, 0.0)
    return jnp.round(v * step).astype(jnp.int32).astype(jnp.int16), top * (1.0 / TOP)


def kernel(
    q_ref, p_ref, reg_ref, pos_ref, breg_ref, mask_ref,
    loss_ref, qg_ref, pg_ref,
    qall, pall, pt, hot, pick, tg, bias, es, wts, mk, lk, ps, st, nrm, side, sidr,
    own, cbuf, crecv, zsend, zrecv, relay, relay_half, zstep, zstepr, qown, qsend, qrecv,
    q_ss, q_rs, h_ss, h_rs, p_ss, p_rs, f_ss, f_rs, n_ss, n_rs, s_ss, s_rs,
    c_ss, c_rs, z_ss, z_rs, y_ss, y_rs, g_ss, g_rs,
):
    blk = lax.axis_index("blk")
    dp = lax.axis_index("dp")
    core = blk % 2
    y = blk // 4
    x = dp % NX
    z = (dp // NX) * 2 + (blk // 2) % 2
    width = q_ref.shape[1]
    rows = q_ref.shape[0]
    nq = PLANE * rows
    scale = 1.0 / math.sqrt(width)

    def device(xx, yy, zz, cc):
        return (yy * 4 + (zz % 2) * 2 + cc, (zz // 2) * NX + xx)

    def plane_peer(slot):
        return device((x + DXY[slot][0]) % NX, (y + DXY[slot][1]) % NY, z, core)

    def z_peer(t):
        return device(x, y, (z + DZ[t]) % NZ, core)

    sibling = device(x, y, z, 1 - core)

    def remote(src, dst, ss, rs, dev):
        return pltpu.make_async_remote_copy(
            src_ref=src, dst_ref=dst, send_sem=ss, recv_sem=rs, device_id=dev, device_id_type=MESH
        )

    barrier = pltpu.get_barrier_semaphore()
    for slot in range(1, PLANE):
        pl.semaphore_signal(barrier, inc=1, device_id=plane_peer(slot), device_id_type=MESH)
    for t in range(1, NZ):
        pl.semaphore_signal(barrier, inc=1, device_id=z_peer(t), device_id_type=MESH)
    pl.semaphore_signal(barrier, inc=1, device_id=sibling, device_id_type=MESH)

    qall[0, :rows, :] = q_ref[...]
    pall[0, :rows, :] = p_ref[...]
    row = lax.broadcasted_iota(jnp.int32, (EXT - rows, rows), 0)
    pos = pos_ref[...]
    small = jnp.where(row == 0, reg_ref[...], jnp.where(row == 1, pos // TILE, pos % TILE)).astype(f32)
    small = small.astype(bf16)
    qall[0, rows:, :rows] = small
    qall[0, rows:, rows:] = small
    pall[0, rows:, :] = jnp.full((EXT - rows, width), breg_ref[0], jnp.int32).astype(f32).astype(bf16)

    pl.semaphore_wait(barrier, PLANE + NZ - 1)

    def q_copy(slot):
        return remote(qall.at[0], qall.at[BACK[slot]], q_ss.at[slot], q_rs.at[BACK[slot]], plane_peer(slot))

    def h_copy(slot, peer):
        a, b = DXY[slot]
        c, d = DXY[peer]
        there = DXY.index(((a - c) % NX, (b - d) % NY))
        part = slice(0, HALF) if b == 0 else slice(HALF, EXT)
        k = 2 * there + (0 if b == 0 else 1)
        return remote(qall.at[slot, part], qall.at[there, part], h_ss.at[k], h_rs.at[k], plane_peer(peer))

    def pass_on(slot):
        a, b = DXY[slot]
        return [h_copy(slot, DXY.index((0, d) if b == 0 else (d, 0))) for d in (1, 3, 2)]

    def p_copy(slot, part, t, k, dz):
        return remote(pall.at[2 * slot, part], pall.at[2 * t, part], p_ss.at[k], p_rs.at[k], z_peer(DZ.index(dz)))

    def p_next(t):
        whole, low, high = slice(0, EXT), slice(0, HALF), slice(HALF, EXT)
        if t == 0:
            return [p_copy(0, whole, ZBACK[k], ZBACK[k], DZ[k]) for k in (3, 4, 1, 2)]
        if DZ[t] == 2:
            return [p_copy(t, low, 7, 7, NZ - 2), p_copy(t, whole, 5, 5, NZ - 1)]
        if DZ[t] == 6:
            return [p_copy(t, high, 7, 8, 2), p_copy(t, whole, 6, 6, 1)]
        return []

    def p_wait(t):
        if t < 7:
            p_copy(0, slice(0, EXT), t, t, 1).wait_recv()
        else:
            p_copy(0, slice(0, HALF), 7, 7, 1).wait_recv()
            p_copy(0, slice(HALF, EXT), 7, 8, 1).wait_recv()

    def f_copy(t):
        return remote(pall.at[2 * t], pall.at[2 * t + 1], f_ss.at[t], f_rs.at[t], sibling)

    for copy in p_next(0):
        copy.start()
    for slot in range(1, AXIS):
        q_copy(slot).start()
    f_copy(0).start()

    ps[...] = jnp.zeros_like(ps)
    region_mask = mask_ref[...].astype(f32).astype(bf16)
    regions = region_mask.shape[0]
    region_ids = lax.broadcasted_iota(jnp.int32, (regions, rows), 0).astype(f32)
    lane_ids = lax.broadcasted_iota(jnp.int32, (8, regions), 1).astype(f32)
    within = lax.broadcasted_iota(jnp.int32, (2 * rows, 256), 0) % rows
    within = within.astype(f32).reshape(2, 16, 8, 256)
    starts = []
    for t in range(NZ):
        for cc in (core, 1 - core):
            b, d = device(x, y, (z + DZ[t]) % NZ, cc)
            starts.append(((b * 16 + d) * TILE).astype(f32))

    def take_queries(slot):
        extra = qall[slot, rows:, :rows].astype(f32)
        lanes = slice(slot * rows, (slot + 1) * rows)
        hot[:, lanes] = (region_ids == extra[0:1]).astype(f32).astype(bf16)
        target = jnp.broadcast_to(extra[1:2] * TILE + extra[2:3], (8, rows))
        for k, start in enumerate(starts):
            tg[k // 2, 8 * (k % 2):8 * (k % 2) + 8, lanes] = target - start

    def take_pair(t):
        pair = pall[2 * t:2 * t + 2, :rows, :].reshape(256, width)
        pt[:, t * 256:(t + 1) * 256] = pair.T
        hots = [
            (lane_ids == pall[2 * t + h, rows:rows + 8, :regions].astype(f32)).astype(f32)
            for h in range(2)
        ]
        pick[16 * t:16 * t + 16, :] = lax.dot_general(
            jnp.concatenate(hots, axis=0).astype(bf16), region_mask, NT, preferred_element_type=f32
        ).astype(bf16)

    def set_bias(first, last, lanes):
        opened = jnp.dot(pick[16 * first:16 * last, :], hot[:, lanes], preferred_element_type=f32)
        for t in range(first, last):
            at = tg[t, :, lanes]
            part = (opened[16 * (t - first):16 * (t - first) + 16] > 0.5) | ((at >= 0.0) & (at < TILE))
            bias[t, :, lanes] = jnp.where(part, 0.0, CLOSED)

    log2e_scale = scale / math.log(2.0)

    def score_tile(t, g):
        lanes = slice(g * 256, (g + 1) * 256)
        pair = pall[2 * t:2 * t + 2, :rows, :].reshape(256, width)
        qg = qall[2 * g:2 * g + 2, :rows, :].reshape(256, width)
        s = lax.dot_general(pair, qg, NT, preferred_element_type=f32).reshape(2, 16, 8, 256)
        target = tg[t, :, lanes].reshape(2, 1, 8, 256)
        ps[:, lanes] += jnp.sum(jnp.where(within == target, s, 0.0), axis=(0, 1))
        s = s * log2e_scale + bias[t, :, lanes].reshape(2, 1, 8, 256)
        high = jnp.max(jnp.max(s, axis=(0, 1)), axis=0, keepdims=True)
        high = jnp.broadcast_to(jnp.maximum(high, FLOOR), (8, 256))
        mk[t, :, lanes] = high
        e = jnp.exp2(s - high)
        lk[t, :, lanes] = jnp.sum(e, axis=(0, 1))
        es[t, :, lanes] = e.reshape(256, 256)

    chunks = nq // 256
    ready = {"t": 0, "g": 0}

    def arrived_queries(slot):
        if slot > 0:
            q_copy(BACK[slot]).wait_recv()
            for copy in pass_on(slot):
                copy.start()
        take_queries(slot)

    def arrived_shard(t):
        p_wait(t)
        for copy in p_next(t):
            copy.start()
        f_copy(t).start()

    def use_pair(t):
        f_copy(t).wait_recv()
        take_pair(t)
        ready["t"] = t + 1
        if ready["g"]:
            set_bias(t, t + 1, slice(0, ready["g"] * 256))
        for g in range(ready["g"]):
            score_tile(t, g)

    def use_chunk(g):
        for slot in (2 * g, 2 * g + 1):
            if slot >= AXIS:
                for half in range(2):
                    part = slice(0, HALF) if half == 0 else slice(HALF, EXT)
                    k = 2 * slot + half
                    remote(qall.at[slot, part], qall.at[slot, part], h_ss.at[k], h_rs.at[k], sibling).wait_recv()
                take_queries(slot)
        ready["g"] = g + 1
        if ready["t"]:
            set_bias(0, ready["t"], slice(g * 256, (g + 1) * 256))
        for t in range(ready["t"]):
            score_tile(t, g)

    steps = (
        (arrived_queries, (0, 1, 2, 3, 4)), (arrived_shard, (3, 4)), (arrived_queries, (5, 6)), (arrived_shard, (1, 2)),
        (use_pair, (0,)), (use_chunk, (0, 1, 2)), (use_pair, (1, 2, 3, 4)), (use_chunk, (3, 4)),
        (arrived_shard, (5, 6)), (use_chunk, (5,)), (arrived_shard, (7,)), (use_pair, (5, 6)), (use_chunk, (6, 7)),
        (use_pair, (7,)),
    )
    for step, items in steps:
        for item in items:
            step(item)

    high = mk[0]
    for t in range(1, NZ):
        high = jnp.maximum(high, mk[t])
    total = jnp.zeros((8, nq), f32)
    for t in range(NZ):
        total += lk[t] * jnp.exp2(mk[t] - high)
    total = jnp.sum(total, axis=0, keepdims=True)
    st[...] = jnp.where(total > 0.0, high[0:1] + jnp.log2(jnp.where(total > 0.0, total, 1.0)), CLOSED)

    def n_copy(slot):
        return remote(st, nrm.at[BACK[slot]], n_ss.at[slot], n_rs.at[BACK[slot]], plane_peer(slot))

    for slot in range(PLANE - 1, 0, -1):
        n_copy(slot).start()
    parts = [st[...]]
    for slot in range(1, PLANE):
        n_copy(BACK[slot]).wait_recv()
        pieces = []
        for a, b in DXY:
            theirs = DXY.index(((a - DXY[slot][0]) % NX, (b - DXY[slot][1]) % NY))
            pieces.append(nrm[slot, :, theirs * rows:(theirs + 1) * rows])
        parts.append(jnp.concatenate(pieces, axis=1))
    high = parts[0]
    for part in parts[1:]:
        high = jnp.maximum(high, part)
    total = jnp.zeros((1, nq), f32)
    for part in parts:
        total += jnp.exp2(part - high)
    log_total = high + jnp.log2(total)
    for t in range(NZ):
        mk[t] = jnp.exp2(mk[t] - log_total)
    lsum = log_total[:, :rows] * math.log(2.0)

    def g_copy(slot):
        return remote(qsend.at[slot], qrecv.at[BACK[slot]], g_ss.at[slot], g_rs.at[BACK[slot]], plane_peer(slot))

    def s_copy(slot):
        return remote(side.at[slot], sidr.at[BACK[slot]], s_ss.at[slot], s_rs.at[BACK[slot]], plane_peer(slot))

    eight = lax.broadcasted_iota(jnp.int32, (8, rows), 0)
    for g in range(chunks - 1, -1, -1):
        lanes = slice(g * 256, (g + 1) * 256)
        for t in range(NZ):
            e = es[t, :, lanes].reshape(2, 16, 8, 256) * mk[t, :, lanes]
            target = tg[t, :, lanes].reshape(2, 1, 8, 256)
            w = jnp.where(within == target, e - 1.0, e).reshape(256, 256).astype(bf16)
            wts[t * 256:(t + 1) * 256, lanes] = w
        grad = jnp.dot(pt[...], wts[:, g * 256:(g + 1) * 256], preferred_element_type=f32)
        for half in range(2):
            slot = 2 * g + half
            piece = grad[:, half * rows:(half + 1) * rows]
            if slot == 0:
                qown[...] = piece
            else:
                qsend[slot], step = quantized(piece)
                found = jnp.sum(ps[:, slot * rows:(slot + 1) * rows], axis=0, keepdims=True)
                side[slot] = jnp.where(eight == 0, found, step)
                g_copy(slot).start()
                s_copy(slot).start()

    def c_copy(t):
        return remote(cbuf.at[t], crecv.at[t], c_ss.at[t], c_rs.at[t], sibling)

    low, high = slice(0, HALF), slice(HALF, rows)
    moves = {
        5: (zsend.at[5], relay.at[0], 1, 5), 6: (zsend.at[6], relay.at[1], 2, 6),
        7: (zsend.at[7, low], relay_half.at[0], 3, 7), 8: (zsend.at[7, high], relay_half.at[1], 4, 8),
        1: (zsend.at[1], zrecv.at[2], 1, 2), 2: (zsend.at[2], zrecv.at[1], 2, 1),
        3: (zsend.at[3], zrecv.at[4], 3, 4), 4: (zsend.at[4], zrecv.at[3], 4, 3),
    }

    def z_copies(k):
        src, dst, peer, there = moves[k]
        return (
            remote(src, dst, z_ss.at[k], z_rs.at[there], z_peer(peer)),
            remote(zstep.at[k], zstepr.at[there], y_ss.at[k], y_rs.at[there], z_peer(peer)),
        )

    def z_send(k):
        for copy in z_copies(k):
            copy.start()

    def z_arrived(there):
        for k in moves:
            if moves[k][3] == there:
                for copy in z_copies(k):
                    copy.wait_recv()

    def combine(t):
        c_copy(t).wait_recv()
        both = own[t] + crecv[t]
        if t in (0, 3, 4):
            own[t] = both
        elif t == 7:
            for k, part in ((7, low), (8, high)):
                zsend[t, part], zstep[k] = quantized(both[part])
                z_send(k)
        else:
            zsend[t], zstep[t] = quantized(both)
            z_send(t)

    order = (5, 6, 7, 1, 2, 3, 4, 0)
    for number, t in enumerate(order):
        grad = jnp.zeros((256, width), f32)
        for g in range(chunks):
            grad += jnp.dot(
                wts[t * 256:(t + 1) * 256, g * 256:(g + 1) * 256],
                qall[2 * g:2 * g + 2, :rows, :].reshape(256, width),
                preferred_element_type=f32,
            )
        own[t] = grad[:rows]
        cbuf[t] = grad[rows:]
        c_copy(t).start()
        if number >= LAG:
            combine(order[number - LAG])
    for t in order[NZ - LAG:]:
        combine(t)

    def decoded(v, step):
        return v.astype(jnp.int32).astype(f32) * step

    for side_no, t in enumerate((3, 4)):
        z_arrived(5 + side_no)
        z_arrived(7 + side_no)
        both = own[t] + decoded(relay[side_no], zstepr[5 + side_no])
        half = decoded(relay_half[side_no], zstepr[7 + side_no])
        halves = [both[:HALF], both[HALF:]]
        halves[side_no] += half
        zsend[t], zstep[t] = quantized(jnp.concatenate(halves, axis=0))
        z_send(t)

    found = jnp.sum(ps[:, :rows], axis=0, keepdims=True)
    grads = qown[...]
    for slot in range(PLANE - 1, 0, -1):
        g_copy(BACK[slot]).wait_recv()
        s_copy(BACK[slot]).wait_recv()
        found += sidr[slot, 0:1]
        grads += decoded(qrecv[slot], sidr[slot, 1:2])
    loss_ref[...] = lsum - found * scale
    qg_ref[...] = grads

    grads = own[0]
    for t in range(1, 5):
        z_arrived(t)
        grads += decoded(zrecv[t], zstepr[t])
    pg_ref[...] = grads

    for t in range(NZ):
        f_copy(t).wait_send()
        c_copy(t).wait_send()
        for copy in p_next(t):
            copy.wait_send()
    for k in moves:
        for copy in z_copies(k):
            copy.wait_send()
    for slot in range(1, PLANE):
        n_copy(slot).wait_send()
        s_copy(slot).wait_send()
        g_copy(slot).wait_send()
    for slot in range(1, AXIS):
        q_copy(slot).wait_send()
        for copy in pass_on(slot):
            copy.wait_send()


def finish(loss_ref, qt_ref, pg_ref, loss_out, qg_out, pg_out):
    scale = 1.0 / math.sqrt(pg_ref.shape[1])
    loss_out[...] = loss_ref[...]
    qg_out[...] = (qt_ref[...] * scale).T
    pg_out[...] = pg_ref[...] * scale


def body(queries, pois, query_region, block_region, region_mask, positive):
    rows, width = queries.shape
    regions = region_mask.shape[0]
    nq = PLANE * rows
    npoi = 2 * NZ * rows
    vmem = pl.BlockSpec(memory_space=pltpu.VMEM)
    dma = pltpu.SemaphoreType.DMA
    loss, query_grad, poi_grad = pl.pallas_call(
        kernel,
        out_shape=(
            jax.ShapeDtypeStruct((1, rows), f32),
            jax.ShapeDtypeStruct((width, rows), f32),
            jax.ShapeDtypeStruct((rows, width), f32),
        ),
        in_specs=[vmem, vmem, vmem, vmem, pl.BlockSpec(memory_space=pltpu.SMEM), vmem],
        out_specs=(vmem, vmem, vmem),
        scratch_shapes=[
            pltpu.VMEM((PLANE, EXT, width), bf16),
            pltpu.VMEM((2 * NZ, EXT, width), bf16),
            pltpu.VMEM((width, npoi), bf16),
            pltpu.VMEM((regions, nq), bf16),
            pltpu.VMEM((16 * NZ, regions), bf16),
            pltpu.VMEM((NZ, 16, nq), f32),
            pltpu.VMEM((NZ, 16, nq), f32),
            pltpu.VMEM((NZ, 2 * rows, nq), f32),
            pltpu.VMEM((npoi, nq), bf16),
            pltpu.VMEM((NZ, 8, nq), f32),
            pltpu.VMEM((NZ, 8, nq), f32),
            pltpu.VMEM((8, nq), f32),
            pltpu.VMEM((1, nq), f32),
            pltpu.VMEM((PLANE, 1, nq), f32),
            pltpu.VMEM((PLANE, 8, rows), f32),
            pltpu.VMEM((PLANE, 8, rows), f32),
            pltpu.VMEM((NZ, rows, width), f32),
            pltpu.VMEM((NZ, rows, width), f32),
            pltpu.VMEM((NZ, rows, width), f32),
            pltpu.VMEM((NZ, rows, width), jnp.int16),
            pltpu.VMEM((5, rows, width), jnp.int16),
            pltpu.VMEM((2, rows, width), jnp.int16),
            pltpu.VMEM((2, HALF, width), jnp.int16),
            pltpu.VMEM((NZ + 1, 1, width), f32),
            pltpu.VMEM((NZ + 1, 1, width), f32),
            pltpu.VMEM((width, rows), f32),
            pltpu.VMEM((PLANE, width, rows), jnp.int16),
            pltpu.VMEM((PLANE, width, rows), jnp.int16),
            dma((PLANE,)), dma((PLANE,)), dma((2 * PLANE,)), dma((2 * PLANE,)), dma((NZ + 1,)), dma((NZ + 1,)),
            dma((NZ,)), dma((NZ,)), dma((PLANE,)), dma((PLANE,)), dma((PLANE,)), dma((PLANE,)),
            dma((NZ,)), dma((NZ,)), dma((NZ + 1,)), dma((NZ + 1,)), dma((NZ + 1,)), dma((NZ + 1,)),
            dma((PLANE,)), dma((PLANE,)),
        ],
        compiler_params=pltpu.CompilerParams(
            collective_id=0, has_side_effects=True, vmem_limit_bytes=56 * 2**20
        ),
    )(
        queries, pois, query_region.reshape(1, rows), positive.reshape(1, rows), block_region, region_mask
    )
    loss, query_grad, poi_grad = pl.pallas_call(
        finish,
        out_shape=(
            jax.ShapeDtypeStruct((1, rows), f32),
            jax.ShapeDtypeStruct((rows, width), f32),
            jax.ShapeDtypeStruct((rows, width), f32),
        ),
        in_specs=[vmem, vmem, vmem],
        out_specs=(vmem, vmem, vmem),
    )(loss, query_grad, poi_grad)
    return (loss.reshape(rows), query_grad, poi_grad)


def solution(mesh):
    in_specs = (
        P(("blk", "dp"), None),
        P(("blk", "dp"), None),
        P(("blk", "dp")),
        P(("blk", "dp")),
        P(),
        P(("blk", "dp")),
    )
    out_specs = (P(("blk", "dp")), P(("blk", "dp"), None), P(("blk", "dp"), None))
    return jax.shard_map(body, mesh=mesh, in_specs=in_specs, out_specs=out_specs, check_vma=False)
```

```python
import math

import jax
import jax.numpy as jnp
from jax import lax
from jax.experimental import pallas as pl
from jax.experimental.pallas import tpu as pltpu
from jax.sharding import PartitionSpec as P

MESH = pl.DeviceIdType.MESH
TILE = 128
EXT = 136
NX, NY, NZ = 4, 4, 8
PLANE = NX * NY
DZ = (0, 1, 7, 2, 6, 3, 5, 4)
ZBACK = tuple(DZ.index((NZ - d) % NZ) for d in DZ)
DXY = (
    (0, 0), (1, 0), (3, 0), (0, 1), (0, 3), (2, 0), (0, 2), (1, 1),
    (3, 3), (1, 3), (3, 1), (2, 1), (2, 3), (1, 2), (3, 2), (2, 2),
)
BACK = tuple(DXY.index(((NX - a) % NX, (NY - b) % NY)) for a, b in DXY)
AXIS = 7
HALF = 64
LAG = 2
CLOSED = -1e30
FLOOR = -1e29
TOP = 32767.0
NT = (((1,), (1,)), ((), ()))
f32, bf16 = jnp.float32, jnp.bfloat16


def quantized(v):
    top = jnp.max(jnp.abs(v.reshape(v.shape[0] // 8, 8, v.shape[1])), axis=0)
    top = jnp.max(top, axis=0, keepdims=True)
    step = jnp.where(top > 0.0, TOP / top, 0.0)
    return jnp.round(v * step).astype(jnp.int32).astype(jnp.int16), top * (1.0 / TOP)


def kernel(
    q_ref, p_ref, reg_ref, pos_ref, breg_ref, mask_ref,
    loss_ref, qg_ref, pg_ref,
    regs, poss, masks, l_ss, qall, pall, pt, hot, pick, tg, bias, es, wts, mk, lk, ps, st, nrm, side, sidr,
    own, cbuf, crecv, zsend, zrecv, relay, relay_half, zstep, zstepr, qown, gsend, grecv, gstep, gstepr, esend, erecv, estep, estepr,
    q_ss, q_rs, h_ss, h_rs, p_ss, p_rs, f_ss, f_rs, n_ss, n_rs, s_ss, s_rs,
    c_ss, c_rs, z_ss, z_rs, y_ss, y_rs, g_ss, g_rs, i_ss, i_rs, e_ss, e_rs, j_ss, j_rs,
):
    blk = lax.axis_index("blk")
    dp = lax.axis_index("dp")
    core = blk % 2
    y = blk // 4
    x = dp % NX
    z = (dp // NX) * 2 + (blk // 2) % 2
    width = q_ref.shape[1]
    rows = q_ref.shape[0]
    nq = PLANE * rows
    scale = 1.0 / math.sqrt(width)

    def device(xx, yy, zz, cc):
        return (yy * 4 + (zz % 2) * 2 + cc, (zz // 2) * NX + xx)

    def plane_peer(slot):
        return device((x + DXY[slot][0]) % NX, (y + DXY[slot][1]) % NY, z, core)

    def z_peer(t):
        return device(x, y, (z + DZ[t]) % NZ, core)

    sibling = device(x, y, z, 1 - core)

    def remote(src, dst, ss, rs, dev):
        return pltpu.make_async_remote_copy(
            src_ref=src, dst_ref=dst, send_sem=ss, recv_sem=rs, device_id=dev, device_id_type=MESH
        )

    loads = [
        pltpu.make_async_copy(src, dst, l_ss.at[k])
        for k, (src, dst) in enumerate((
            (reg_ref, regs), (pos_ref, poss), (mask_ref, masks),
            (q_ref, qall.at[0, :rows, :]), (p_ref, pall.at[0, :rows, :]),
        ))
    ]
    for load in loads:
        load.start()
    barrier = pltpu.get_barrier_semaphore()
    near = [plane_peer(slot) for slot in range(1, PLANE)] + [z_peer(t) for t in range(1, 5)] + [sibling]
    for peer in near:
        pl.semaphore_signal(barrier, inc=1, device_id=peer, device_id_type=MESH)

    for load in loads:
        load.wait()
    row = lax.broadcasted_iota(jnp.int32, (EXT - rows, rows), 0)
    pos = poss[...]
    small = jnp.where(row == 0, regs[...], jnp.where(row == 1, pos // TILE, pos % TILE)).astype(f32)
    small = small.astype(bf16)
    qall[0, rows:, :rows] = small
    qall[0, rows:, rows:] = small
    pall[0, rows:, :] = jnp.full((EXT - rows, width), breg_ref[0], jnp.int32).astype(f32).astype(bf16)

    pl.semaphore_wait(barrier, len(near))

    def q_copy(slot):
        return remote(qall.at[0], qall.at[BACK[slot]], q_ss.at[slot], q_rs.at[BACK[slot]], plane_peer(slot))

    def h_copy(slot, peer):
        a, b = DXY[slot]
        c, d = DXY[peer]
        there = DXY.index(((a - c) % NX, (b - d) % NY))
        part = slice(0, HALF) if b == 0 else slice(HALF, EXT)
        k = 2 * there + (0 if b == 0 else 1)
        return remote(qall.at[slot, part], qall.at[there, part], h_ss.at[k], h_rs.at[k], plane_peer(peer))

    def pass_on(slot):
        a, b = DXY[slot]
        return [h_copy(slot, DXY.index((0, d) if b == 0 else (d, 0))) for d in (1, 3, 2)]

    def p_copy(slot, part, t, k, dz):
        return remote(pall.at[2 * slot, part], pall.at[2 * t, part], p_ss.at[k], p_rs.at[k], z_peer(DZ.index(dz)))

    def p_next(t):
        whole, low, high = slice(0, EXT), slice(0, HALF), slice(HALF, EXT)
        if t == 0:
            return [p_copy(0, whole, ZBACK[k], ZBACK[k], DZ[k]) for k in (3, 4, 1, 2)]
        if DZ[t] == 2:
            return [p_copy(t, low, 7, 7, NZ - 2), p_copy(t, whole, 5, 5, NZ - 1)]
        if DZ[t] == 6:
            return [p_copy(t, high, 7, 8, 2), p_copy(t, whole, 6, 6, 1)]
        return []

    def p_wait(t):
        if t < 7:
            p_copy(0, slice(0, EXT), t, t, 1).wait_recv()
        else:
            p_copy(0, slice(0, HALF), 7, 7, 1).wait_recv()
            p_copy(0, slice(HALF, EXT), 7, 8, 1).wait_recv()

    def f_copy(t):
        return remote(pall.at[2 * t], pall.at[2 * t + 1], f_ss.at[t], f_rs.at[t], sibling)

    for copy in p_next(0):
        copy.start()
    for slot in range(1, AXIS):
        q_copy(slot).start()
    f_copy(0).start()

    ps[...] = jnp.zeros_like(ps)
    region_mask = masks[...].astype(f32).astype(bf16)
    regions = region_mask.shape[0]
    region_ids = lax.broadcasted_iota(jnp.int32, (regions, rows), 0).astype(f32)
    lane_ids = lax.broadcasted_iota(jnp.int32, (8, regions), 1).astype(f32)
    within = lax.broadcasted_iota(jnp.int32, (2 * rows, 256), 0) % rows
    within = within.astype(f32).reshape(2, 16, 8, 256)
    starts = []
    for t in range(NZ):
        for cc in (core, 1 - core):
            b, d = device(x, y, (z + DZ[t]) % NZ, cc)
            starts.append(((b * 16 + d) * TILE).astype(f32))

    def take_queries(slot):
        extra = qall[slot, rows:, :rows].astype(f32)
        lanes = slice(slot * rows, (slot + 1) * rows)
        hot[:, lanes] = (region_ids == extra[0:1]).astype(f32).astype(bf16)
        target = jnp.broadcast_to(extra[1:2] * TILE + extra[2:3], (8, rows))
        for k, start in enumerate(starts):
            tg[k // 2, 8 * (k % 2):8 * (k % 2) + 8, lanes] = target - start

    def take_pair(t):
        pair = pall[2 * t:2 * t + 2, :rows, :].reshape(256, width)
        pt[:, t * 256:(t + 1) * 256] = pair.T
        hots = [
            (lane_ids == pall[2 * t + h, rows:rows + 8, :regions].astype(f32)).astype(f32)
            for h in range(2)
        ]
        pick[16 * t:16 * t + 16, :] = lax.dot_general(
            jnp.concatenate(hots, axis=0).astype(bf16), region_mask, NT, preferred_element_type=f32
        ).astype(bf16)

    def set_bias(first, last, lanes):
        opened = jnp.dot(pick[16 * first:16 * last, :], hot[:, lanes], preferred_element_type=f32)
        for t in range(first, last):
            at = tg[t, :, lanes]
            part = (opened[16 * (t - first):16 * (t - first) + 16] > 0.5) | ((at >= 0.0) & (at < TILE))
            bias[t, :, lanes] = jnp.where(part, 0.0, CLOSED)

    log2e_scale = scale / math.log(2.0)

    def score_tile(t, g):
        lanes = slice(g * 256, (g + 1) * 256)
        pair = pall[2 * t:2 * t + 2, :rows, :].reshape(256, width)
        qg = qall[2 * g:2 * g + 2, :rows, :].reshape(256, width)
        s = lax.dot_general(pair, qg, NT, preferred_element_type=f32).reshape(2, 16, 8, 256)
        target = tg[t, :, lanes].reshape(2, 1, 8, 256)
        ps[:, lanes] += jnp.sum(jnp.where(within == target, s, 0.0), axis=(0, 1))
        s = s * log2e_scale + bias[t, :, lanes].reshape(2, 1, 8, 256)
        high = jnp.max(jnp.max(s, axis=(0, 1)), axis=0, keepdims=True)
        high = jnp.broadcast_to(jnp.maximum(high, FLOOR), (8, 256))
        mk[t, :, lanes] = high
        e = jnp.exp2(s - high)
        lk[t, :, lanes] = jnp.sum(e, axis=(0, 1))
        es[t, :, lanes] = e.reshape(256, 256)

    chunks = nq // 256
    ready = {"t": 0, "g": 0}

    def arrived_queries(slot):
        if slot > 0:
            q_copy(BACK[slot]).wait_recv()
            for copy in pass_on(slot):
                copy.start()
        take_queries(slot)

    def arrived_shard(t):
        p_wait(t)
        for copy in p_next(t):
            copy.start()
        f_copy(t).start()

    def use_pair(t):
        f_copy(t).wait_recv()
        take_pair(t)
        ready["t"] = t + 1
        if ready["g"]:
            set_bias(t, t + 1, slice(0, ready["g"] * 256))
        for g in range(ready["g"]):
            score_tile(t, g)

    def use_chunk(g):
        for slot in (2 * g, 2 * g + 1):
            if slot >= AXIS:
                for half in range(2):
                    part = slice(0, HALF) if half == 0 else slice(HALF, EXT)
                    k = 2 * slot + half
                    remote(qall.at[slot, part], qall.at[slot, part], h_ss.at[k], h_rs.at[k], sibling).wait_recv()
                take_queries(slot)
        ready["g"] = g + 1
        if ready["t"]:
            set_bias(0, ready["t"], slice(g * 256, (g + 1) * 256))
        for t in range(ready["t"]):
            score_tile(t, g)

    steps = (
        (arrived_queries, (0, 1, 2, 3, 4)), (arrived_shard, (3, 4)), (arrived_queries, (5, 6)), (arrived_shard, (1, 2)),
        (use_pair, (0,)), (use_chunk, (0, 1, 2)), (use_pair, (1, 2, 3, 4)), (use_chunk, (3, 4)),
        (arrived_shard, (5, 6)), (use_chunk, (5,)), (arrived_shard, (7,)), (use_pair, (5, 6)), (use_chunk, (6, 7)),
        (use_pair, (7,)),
    )
    for step, items in steps:
        for item in items:
            step(item)

    high = mk[0]
    for t in range(1, NZ):
        high = jnp.maximum(high, mk[t])
    total = jnp.zeros((8, nq), f32)
    for t in range(NZ):
        total += lk[t] * jnp.exp2(mk[t] - high)
    total = jnp.sum(total, axis=0, keepdims=True)
    st[...] = jnp.where(total > 0.0, high[0:1] + jnp.log2(jnp.where(total > 0.0, total, 1.0)), CLOSED)

    def n_copy(slot):
        return remote(st, nrm.at[BACK[slot]], n_ss.at[slot], n_rs.at[BACK[slot]], plane_peer(slot))

    def s_copy(slot):
        return remote(side.at[slot], sidr.at[BACK[slot]], s_ss.at[slot], s_rs.at[BACK[slot]], plane_peer(slot))

    for slot in range(PLANE - 1, 0, -1):
        n_copy(slot).start()
    for slot in range(PLANE - 1, 0, -1):
        side[slot] = jnp.sum(ps[:, slot * rows:(slot + 1) * rows], axis=0, keepdims=True)
        s_copy(slot).start()
    parts = [st[...]]
    for slot in range(1, PLANE):
        n_copy(BACK[slot]).wait_recv()
        pieces = []
        for a, b in DXY:
            theirs = DXY.index(((a - DXY[slot][0]) % NX, (b - DXY[slot][1]) % NY))
            pieces.append(nrm[slot, :, theirs * rows:(theirs + 1) * rows])
        parts.append(jnp.concatenate(pieces, axis=1))
    high = parts[0]
    for part in parts[1:]:
        high = jnp.maximum(high, part)
    total = jnp.zeros((1, nq), f32)
    for part in parts:
        total += jnp.exp2(part - high)
    log_total = high + jnp.log2(total)
    for t in range(NZ):
        mk[t] = jnp.exp2(mk[t] - log_total)
    lsum = log_total[:, :rows] * math.log(2.0)

    def c_copy(t):
        return remote(cbuf.at[t], crecv.at[t], c_ss.at[t], c_rs.at[t], sibling)

    low, high = slice(0, HALF), slice(HALF, rows)
    moves = {
        5: (zsend.at[5], relay.at[0], 1, 5), 6: (zsend.at[6], relay.at[1], 2, 6),
        7: (zsend.at[7, low], relay_half.at[0], 3, 7), 8: (zsend.at[7, high], relay_half.at[1], 4, 8),
        1: (zsend.at[1], zrecv.at[2], 1, 2), 2: (zsend.at[2], zrecv.at[1], 2, 1),
        3: (zsend.at[3], zrecv.at[4], 3, 4), 4: (zsend.at[4], zrecv.at[3], 4, 3),
    }

    def z_copies(k):
        src, dst, peer, there = moves[k]
        return (
            remote(src, dst, z_ss.at[k], z_rs.at[there], z_peer(peer)),
            remote(zstep.at[k], zstepr.at[there], y_ss.at[k], y_rs.at[there], z_peer(peer)),
        )

    def z_send(k):
        for copy in z_copies(k):
            copy.start()

    def z_arrived(there):
        for k in moves:
            if moves[k][3] == there:
                for copy in z_copies(k):
                    copy.wait_recv()

    def combine(t):
        c_copy(t).wait_recv()
        both = own[t] + crecv[t]
        if t in (0, 3, 4):
            own[t] = both
        elif t == 7:
            for k, part in ((7, low), (8, high)):
                zsend[t, part], zstep[k] = quantized(both[part])
                z_send(k)
        else:
            zsend[t], zstep[t] = quantized(both)
            z_send(t)

    def line(way, d):
        return DXY.index((d, 0) if way == 0 else (0, d))

    def g_copies(way, d, e):
        k, there = 16 * way + 4 * d + e, 16 * way + 4 * ((4 - d) % 4) + e
        peer = plane_peer(line(way, d))
        return (
            remote(gsend.at[k], grecv.at[there], g_ss.at[k], g_rs.at[there], peer),
            remote(gstep.at[k], gstepr.at[there], i_ss.at[k], i_rs.at[there], peer),
        )

    def e_copies(way, d):
        k, there = 4 * way + d, 4 * way + (4 - d) % 4
        peer = plane_peer(line(1 - way, d))
        return (
            remote(esend.at[k], erecv.at[there], e_ss.at[k], e_rs.at[there], peer),
            remote(estep.at[k], estepr.at[there], j_ss.at[k], j_rs.at[there], peer),
        )

    def set_weights(t, g):
        lanes = slice(g * 256, (g + 1) * 256)
        e = es[t, :, lanes].reshape(2, 16, 8, 256) * mk[t, :, lanes]
        target = tg[t, :, lanes].reshape(2, 1, 8, 256)
        w = jnp.where(within == target, e - 1.0, e).reshape(256, 256).astype(bf16)
        wts[t * 256:(t + 1) * 256, lanes] = w

    def poi_step(t):
        grad = jnp.zeros((256, width), f32)
        for g in range(chunks):
            grad += jnp.dot(
                wts[t * 256:(t + 1) * 256, g * 256:(g + 1) * 256],
                qall[2 * g:2 * g + 2, :rows, :].reshape(256, width),
                preferred_element_type=f32,
            )
        own[t] = grad[:rows]
        cbuf[t] = grad[rows:]
        c_copy(t).start()

    def query_step(g):
        grad = jnp.dot(pt[...], wts[:, g * 256:(g + 1) * 256], preferred_element_type=f32)
        for half in range(2):
            slot = 2 * g + half
            piece = grad[:, half * rows:(half + 1) * rows]
            if slot < AXIS:
                qown[slot] = piece
            for way in range(2):
                d, e = DXY[slot] if way == 0 else DXY[slot][::-1]
                if d > 0:
                    k = 16 * way + 4 * d + e
                    gsend[k], gstep[k] = quantized(piece[way * rows:(way + 1) * rows])
                    for copy in g_copies(way, d, e):
                        copy.start()

    first = (7, 5, 6)
    later = (1, 2, 3, 4, 0)
    for t in first:
        for g in range(chunks):
            set_weights(t, g)
        poi_step(t)
        if t != first[0]:
            combine(first[first.index(t) - 1])
    waiting = [first[-1]]
    for g in range(chunks - 1, -1, -1):
        for t in later:
            set_weights(t, g)
        query_step(g)
        if waiting:
            combine(waiting.pop(0))
    for number, t in enumerate(later):
        poi_step(t)
        if number >= LAG:
            combine(later[number - LAG])
    for t in later[len(later) - LAG:]:
        combine(t)

    def decoded(v, step):
        return v.astype(jnp.int32).astype(f32) * step

    def add_line(way, e):
        mine = qown[line(1 - way, e), way * rows:(way + 1) * rows]
        for d in (1, 3, 2):
            for copy in g_copies(way, (4 - d) % 4, e):
                copy.wait_recv()
            k = 16 * way + 4 * d + e
            mine += decoded(grecv[k], gstepr[k])
        return mine

    def pass_line(way, e):
        k = 4 * way + e
        esend[k], estep[k] = quantized(add_line(way, e))
        for copy in e_copies(way, e):
            copy.start()

    pass_line(0, 2)
    pass_line(1, 2)
    for side_no, t in enumerate((3, 4)):
        z_arrived(5 + side_no)
        z_arrived(7 + side_no)
        both = own[t] + decoded(relay[side_no], zstepr[5 + side_no])
        half = decoded(relay_half[side_no], zstepr[7 + side_no])
        halves = [both[:HALF], both[HALF:]]
        halves[side_no] += half
        zsend[t], zstep[t] = quantized(jnp.concatenate(halves, axis=0))
        z_send(t)

    for e in (1, 3):
        pass_line(0, e)
        pass_line(1, e)

    found = jnp.sum(ps[:, :rows], axis=0, keepdims=True)
    for slot in range(1, PLANE):
        s_copy(BACK[slot]).wait_recv()
        found += sidr[slot]
    loss_ref[...] = lsum - found * scale
    for way in range(2):
        grads = add_line(way, 0)
        for d in (2, 1, 3):
            for copy in e_copies(way, (4 - d) % 4):
                copy.wait_recv()
            grads += decoded(erecv[4 * way + d], estepr[4 * way + d])
        qg_ref[way * rows:(way + 1) * rows, :] = grads

    grads = own[0]
    for t in range(1, 5):
        z_arrived(t)
        grads += decoded(zrecv[t], zstepr[t])
    pg_ref[...] = grads

    for t in range(NZ):
        f_copy(t).wait_send()
        c_copy(t).wait_send()
        for copy in p_next(t):
            copy.wait_send()
    for k in moves:
        for copy in z_copies(k):
            copy.wait_send()
    for slot in range(1, PLANE):
        n_copy(slot).wait_send()
        s_copy(slot).wait_send()
    for way in range(2):
        for d in range(1, 4):
            for copy in e_copies(way, d):
                copy.wait_send()
            for e in range(4):
                for copy in g_copies(way, d, e):
                    copy.wait_send()
    for slot in range(1, AXIS):
        q_copy(slot).wait_send()
        for copy in pass_on(slot):
            copy.wait_send()


def finish(loss_ref, qt_ref, pg_ref, loss_out, qg_out, pg_out):
    scale = 1.0 / math.sqrt(pg_ref.shape[1])
    loss_out[...] = loss_ref[...]
    qg_out[...] = (qt_ref[...] * scale).T
    pg_out[...] = pg_ref[...] * scale


def body(queries, pois, query_region, block_region, region_mask, positive):
    rows, width = queries.shape
    regions = region_mask.shape[0]
    nq = PLANE * rows
    npoi = 2 * NZ * rows
    vmem = pl.BlockSpec(memory_space=pltpu.VMEM)
    hbm = pl.BlockSpec(memory_space=pl.ANY)
    dma = pltpu.SemaphoreType.DMA
    loss, query_grad, poi_grad = pl.pallas_call(
        kernel,
        out_shape=(
            jax.ShapeDtypeStruct((1, rows), f32),
            jax.ShapeDtypeStruct((width, rows), f32),
            jax.ShapeDtypeStruct((rows, width), f32),
        ),
        in_specs=[hbm, hbm, hbm, hbm, pl.BlockSpec(memory_space=pltpu.SMEM), hbm],
        out_specs=(vmem, vmem, vmem),
        scratch_shapes=[
            pltpu.VMEM((1, rows), jnp.int32),
            pltpu.VMEM((1, rows), jnp.int32),
            pltpu.VMEM((regions, regions), jnp.int32),
            dma((5,)),
            pltpu.VMEM((PLANE, EXT, width), bf16),
            pltpu.VMEM((2 * NZ, EXT, width), bf16),
            pltpu.VMEM((width, npoi), bf16),
            pltpu.VMEM((regions, nq), bf16),
            pltpu.VMEM((16 * NZ, regions), bf16),
            pltpu.VMEM((NZ, 16, nq), f32),
            pltpu.VMEM((NZ, 16, nq), f32),
            pltpu.VMEM((NZ, 2 * rows, nq), f32),
            pltpu.VMEM((npoi, nq), bf16),
            pltpu.VMEM((NZ, 8, nq), f32),
            pltpu.VMEM((NZ, 8, nq), f32),
            pltpu.VMEM((8, nq), f32),
            pltpu.VMEM((1, nq), f32),
            pltpu.VMEM((PLANE, 1, nq), f32),
            pltpu.VMEM((PLANE, 1, rows), f32),
            pltpu.VMEM((PLANE, 1, rows), f32),
            pltpu.VMEM((NZ, rows, width), f32),
            pltpu.VMEM((NZ, rows, width), f32),
            pltpu.VMEM((NZ, rows, width), f32),
            pltpu.VMEM((NZ, rows, width), jnp.int16),
            pltpu.VMEM((5, rows, width), jnp.int16),
            pltpu.VMEM((2, rows, width), jnp.int16),
            pltpu.VMEM((2, HALF, width), jnp.int16),
            pltpu.VMEM((NZ + 1, 1, width), f32),
            pltpu.VMEM((NZ + 1, 1, width), f32),
            pltpu.VMEM((AXIS, width, rows), f32),
            pltpu.VMEM((32, width // 2, rows), jnp.int16),
            pltpu.VMEM((32, width // 2, rows), jnp.int16),
            pltpu.VMEM((32, 1, rows), f32),
            pltpu.VMEM((32, 1, rows), f32),
            pltpu.VMEM((8, width // 2, rows), jnp.int16),
            pltpu.VMEM((8, width // 2, rows), jnp.int16),
            pltpu.VMEM((8, 1, rows), f32),
            pltpu.VMEM((8, 1, rows), f32),
            dma((PLANE,)), dma((PLANE,)), dma((2 * PLANE,)), dma((2 * PLANE,)), dma((NZ + 1,)), dma((NZ + 1,)),
            dma((NZ,)), dma((NZ,)), dma((PLANE,)), dma((PLANE,)), dma((PLANE,)), dma((PLANE,)),
            dma((NZ,)), dma((NZ,)), dma((NZ + 1,)), dma((NZ + 1,)), dma((NZ + 1,)), dma((NZ + 1,)),
            dma((32,)), dma((32,)), dma((32,)), dma((32,)), dma((8,)), dma((8,)), dma((8,)), dma((8,)),
        ],
        compiler_params=pltpu.CompilerParams(
            collective_id=0, has_side_effects=True, vmem_limit_bytes=56 * 2**20
        ),
    )(
        queries, pois, query_region.reshape(1, rows), positive.reshape(1, rows), block_region, region_mask
    )
    loss, query_grad, poi_grad = pl.pallas_call(
        finish,
        out_shape=(
            jax.ShapeDtypeStruct((1, rows), f32),
            jax.ShapeDtypeStruct((rows, width), f32),
            jax.ShapeDtypeStruct((rows, width), f32),
        ),
        in_specs=[vmem, vmem, vmem],
        out_specs=(vmem, vmem, vmem),
    )(loss, query_grad, poi_grad)
    return (loss.reshape(rows), query_grad, poi_grad)


def solution(mesh):
    in_specs = (
        P(("blk", "dp"), None),
        P(("blk", "dp"), None),
        P(("blk", "dp")),
        P(("blk", "dp")),
        P(),
        P(("blk", "dp")),
    )
    out_specs = (P(("blk", "dp")), P(("blk", "dp"), None), P(("blk", "dp"), None))
    return jax.shard_map(body, mesh=mesh, in_specs=in_specs, out_specs=out_specs, check_vma=False)
```

```python
import math

import jax
import jax.numpy as jnp
from jax import lax
from jax.experimental import pallas as pl
from jax.experimental.pallas import tpu as pltpu
from jax.sharding import PartitionSpec as P

MESH = pl.DeviceIdType.MESH
TILE = 128
EXT = 136
NX, NY, NZ = 4, 4, 8
PLANE = NX * NY
DZ = (0, 1, 7, 2, 6, 3, 5, 4)
ZBACK = tuple(DZ.index((NZ - d) % NZ) for d in DZ)
DXY = (
    (0, 0), (1, 0), (3, 0), (0, 1), (0, 3), (2, 0), (0, 2), (1, 1),
    (3, 3), (1, 3), (3, 1), (2, 1), (2, 3), (1, 2), (3, 2), (2, 2),
)
BACK = tuple(DXY.index(((NX - a) % NX, (NY - b) % NY)) for a, b in DXY)
AXIS = 7
HALF = 64
LAG = 2
CLOSED = -1e30
FLOOR = -1e29
TOP = 32767.0
NT = (((1,), (1,)), ((), ()))
f32, bf16 = jnp.float32, jnp.bfloat16


def quantized(v):
    top = jnp.max(jnp.abs(v.reshape(v.shape[0] // 8, 8, v.shape[1])), axis=0)
    top = jnp.max(top, axis=0, keepdims=True)
    step = jnp.where(top > 0.0, TOP / top, 0.0)
    return jnp.round(v * step).astype(jnp.int32).astype(jnp.int16), top * (1.0 / TOP)


def kernel(
    q_ref, p_ref, reg_ref, pos_ref, breg_ref, mask_ref,
    loss_ref, qg_ref, pg_ref,
    regs, poss, masks, l_ss, qall, pall, pt, hot, pick, tg, bias, es, wts, mk, lk, ps, st, nrm, side, sidr,
    own, cbuf, crecv, zsend, zrecv, relay, relay_half, zstep, zstepr, qown, gsend, grecv, gstep, gstepr, esend, erecv, estep, estepr,
    q_ss, q_rs, h_ss, h_rs, p_ss, p_rs, f_ss, f_rs, n_ss, n_rs, s_ss, s_rs,
    c_ss, c_rs, z_ss, z_rs, y_ss, y_rs, g_ss, g_rs, i_ss, i_rs, e_ss, e_rs, j_ss, j_rs,
):
    blk = lax.axis_index("blk")
    dp = lax.axis_index("dp")
    core = blk % 2
    y = blk // 4
    x = dp % NX
    z = (dp // NX) * 2 + (blk // 2) % 2
    width = q_ref.shape[1]
    rows = q_ref.shape[0]
    nq = PLANE * rows
    scale = 1.0 / math.sqrt(width)

    def device(xx, yy, zz, cc):
        return (yy * 4 + (zz % 2) * 2 + cc, (zz // 2) * NX + xx)

    def plane_peer(slot):
        return device((x + DXY[slot][0]) % NX, (y + DXY[slot][1]) % NY, z, core)

    def z_peer(t):
        return device(x, y, (z + DZ[t]) % NZ, core)

    sibling = device(x, y, z, 1 - core)

    def remote(src, dst, ss, rs, dev):
        return pltpu.make_async_remote_copy(
            src_ref=src, dst_ref=dst, send_sem=ss, recv_sem=rs, device_id=dev, device_id_type=MESH
        )

    loads = [
        pltpu.make_async_copy(src, dst, l_ss.at[k])
        for k, (src, dst) in enumerate((
            (reg_ref, regs), (pos_ref, poss), (mask_ref, masks),
            (q_ref, qall.at[0, :rows, :]), (p_ref, pall.at[0, :rows, :]),
        ))
    ]
    for load in loads:
        load.start()
    barrier = pltpu.get_barrier_semaphore()
    near = [plane_peer(slot) for slot in range(1, PLANE)] + [z_peer(t) for t in range(1, 5)] + [sibling]
    for peer in near:
        pl.semaphore_signal(barrier, inc=1, device_id=peer, device_id_type=MESH)

    for load in loads:
        load.wait()
    row = lax.broadcasted_iota(jnp.int32, (EXT - rows, rows), 0)
    pos = poss[...]
    small = jnp.where(row == 0, regs[...], jnp.where(row == 1, pos // TILE, pos % TILE)).astype(f32)
    small = small.astype(bf16)
    qall[0, rows:, :rows] = small
    qall[0, rows:, rows:] = small
    pall[0, rows:, :] = jnp.full((EXT - rows, width), breg_ref[0], jnp.int32).astype(f32).astype(bf16)

    pl.semaphore_wait(barrier, len(near))

    def q_copy(slot):
        return remote(qall.at[0], qall.at[BACK[slot]], q_ss.at[slot], q_rs.at[BACK[slot]], plane_peer(slot))

    def h_copy(slot, peer):
        a, b = DXY[slot]
        c, d = DXY[peer]
        there = DXY.index(((a - c) % NX, (b - d) % NY))
        part = slice(0, HALF) if b == 0 else slice(HALF, EXT)
        k = 2 * there + (0 if b == 0 else 1)
        return remote(qall.at[slot, part], qall.at[there, part], h_ss.at[k], h_rs.at[k], plane_peer(peer))

    def pass_on(slot):
        a, b = DXY[slot]
        return [h_copy(slot, DXY.index((0, d) if b == 0 else (d, 0))) for d in (1, 3, 2)]

    def p_copy(slot, part, t, k, dz):
        return remote(pall.at[2 * slot, part], pall.at[2 * t, part], p_ss.at[k], p_rs.at[k], z_peer(DZ.index(dz)))

    def p_next(t):
        whole, low, high = slice(0, EXT), slice(0, HALF), slice(HALF, EXT)
        if t == 0:
            return [p_copy(0, whole, ZBACK[k], ZBACK[k], DZ[k]) for k in (3, 4, 1, 2)]
        if DZ[t] == 2:
            return [p_copy(t, low, 7, 7, NZ - 2), p_copy(t, whole, 5, 5, NZ - 1)]
        if DZ[t] == 6:
            return [p_copy(t, high, 7, 8, 2), p_copy(t, whole, 6, 6, 1)]
        return []

    def p_wait(t):
        if t < 7:
            p_copy(0, slice(0, EXT), t, t, 1).wait_recv()
        else:
            p_copy(0, slice(0, HALF), 7, 7, 1).wait_recv()
            p_copy(0, slice(HALF, EXT), 7, 8, 1).wait_recv()

    def f_copy(t):
        return remote(pall.at[2 * t], pall.at[2 * t + 1], f_ss.at[t], f_rs.at[t], sibling)

    for copy in p_next(0):
        copy.start()
    for slot in range(1, AXIS):
        q_copy(slot).start()
    f_copy(0).start()

    ps[...] = jnp.zeros_like(ps)
    region_mask = masks[...].astype(f32).astype(bf16)
    regions = region_mask.shape[0]
    region_ids = lax.broadcasted_iota(jnp.int32, (regions, rows), 0).astype(f32)
    lane_ids = lax.broadcasted_iota(jnp.int32, (8, regions), 1).astype(f32)
    within = lax.broadcasted_iota(jnp.int32, (2 * rows, 256), 0) % rows
    within = within.astype(f32).reshape(2, 16, 8, 256)
    starts = []
    for t in range(NZ):
        for cc in (core, 1 - core):
            b, d = device(x, y, (z + DZ[t]) % NZ, cc)
            starts.append(((b * 16 + d) * TILE).astype(f32))

    def take_queries(slot):
        extra = qall[slot, rows:, :rows].astype(f32)
        lanes = slice(slot * rows, (slot + 1) * rows)
        hot[:, lanes] = (region_ids == extra[0:1]).astype(f32).astype(bf16)
        target = jnp.broadcast_to(extra[1:2] * TILE + extra[2:3], (8, rows))
        for k, start in enumerate(starts):
            tg[k // 2, 8 * (k % 2):8 * (k % 2) + 8, lanes] = target - start

    def take_pair(t):
        pair = pall[2 * t:2 * t + 2, :rows, :].reshape(256, width)
        pt[:, t * 256:(t + 1) * 256] = pair.T
        hots = [
            (lane_ids == pall[2 * t + h, rows:rows + 8, :regions].astype(f32)).astype(f32)
            for h in range(2)
        ]
        pick[16 * t:16 * t + 16, :] = lax.dot_general(
            jnp.concatenate(hots, axis=0).astype(bf16), region_mask, NT, preferred_element_type=f32
        ).astype(bf16)

    def set_bias(first, last, lanes):
        opened = jnp.dot(pick[16 * first:16 * last, :], hot[:, lanes], preferred_element_type=f32)
        for t in range(first, last):
            at = tg[t, :, lanes]
            part = (opened[16 * (t - first):16 * (t - first) + 16] > 0.5) | ((at >= 0.0) & (at < TILE))
            bias[t, :, lanes] = jnp.where(part, 0.0, CLOSED)

    log2e_scale = scale / math.log(2.0)

    def score_tile(t, g):
        lanes = slice(g * 256, (g + 1) * 256)
        pair = pall[2 * t:2 * t + 2, :rows, :].reshape(256, width)
        qg = qall[2 * g:2 * g + 2, :rows, :].reshape(256, width)
        s = lax.dot_general(pair, qg, NT, preferred_element_type=f32).reshape(2, 16, 8, 256)
        target = tg[t, :, lanes].reshape(2, 1, 8, 256)
        ps[:, lanes] += jnp.sum(jnp.where(within == target, s, 0.0), axis=(0, 1))
        s = s * log2e_scale + bias[t, :, lanes].reshape(2, 1, 8, 256)
        high = jnp.max(jnp.max(s, axis=(0, 1)), axis=0, keepdims=True)
        high = jnp.broadcast_to(jnp.maximum(high, FLOOR), (8, 256))
        mk[t, :, lanes] = high
        e = jnp.exp2(s - high)
        lk[t, :, lanes] = jnp.sum(e, axis=(0, 1))
        es[t, :, lanes] = e.reshape(256, 256)

    chunks = nq // 256
    ready = {"t": 0, "g": 0}

    def arrived_queries(slot):
        if slot > 0:
            q_copy(BACK[slot]).wait_recv()
            for copy in pass_on(slot):
                copy.start()
        take_queries(slot)

    def arrived_shard(t):
        p_wait(t)
        for copy in p_next(t):
            copy.start()
        f_copy(t).start()

    def use_pair(t):
        f_copy(t).wait_recv()
        take_pair(t)
        ready["t"] = t + 1
        if ready["g"]:
            set_bias(t, t + 1, slice(0, ready["g"] * 256))
        for g in range(ready["g"]):
            score_tile(t, g)

    def use_chunk(g):
        for slot in (2 * g, 2 * g + 1):
            if slot >= AXIS:
                for half in range(2):
                    part = slice(0, HALF) if half == 0 else slice(HALF, EXT)
                    k = 2 * slot + half
                    remote(qall.at[slot, part], qall.at[slot, part], h_ss.at[k], h_rs.at[k], sibling).wait_recv()
                take_queries(slot)
        ready["g"] = g + 1
        if ready["t"]:
            set_bias(0, ready["t"], slice(g * 256, (g + 1) * 256))
        for t in range(ready["t"]):
            score_tile(t, g)

    steps = (
        (arrived_queries, (0, 1, 2, 3, 4)), (arrived_shard, (3, 4)), (arrived_queries, (5, 6)), (arrived_shard, (1, 2)),
        (use_pair, (0,)), (use_chunk, (0, 1, 2)), (use_pair, (1, 2, 3, 4)), (use_chunk, (3, 4)),
        (arrived_shard, (5, 6)), (use_chunk, (5,)), (arrived_shard, (7,)), (use_pair, (5, 6)), (use_chunk, (6, 7)),
        (use_pair, (7,)),
    )
    for step, items in steps:
        for item in items:
            step(item)

    high = mk[0]
    for t in range(1, NZ):
        high = jnp.maximum(high, mk[t])
    total = jnp.zeros((8, nq), f32)
    for t in range(NZ):
        total += lk[t] * jnp.exp2(mk[t] - high)
    total = jnp.sum(total, axis=0, keepdims=True)
    st[...] = jnp.where(total > 0.0, high[0:1] + jnp.log2(jnp.where(total > 0.0, total, 1.0)), CLOSED)

    def n_copy(slot):
        return remote(st, nrm.at[BACK[slot]], n_ss.at[slot], n_rs.at[BACK[slot]], plane_peer(slot))

    def s_copy(slot):
        return remote(side.at[slot], sidr.at[BACK[slot]], s_ss.at[slot], s_rs.at[BACK[slot]], plane_peer(slot))

    for slot in range(PLANE - 1, 0, -1):
        n_copy(slot).start()
    for slot in range(PLANE - 1, 0, -1):
        side[slot] = jnp.sum(ps[:, slot * rows:(slot + 1) * rows], axis=0, keepdims=True)
        s_copy(slot).start()
    parts = [st[...]]
    for slot in range(1, PLANE):
        n_copy(BACK[slot]).wait_recv()
        pieces = []
        for a, b in DXY:
            theirs = DXY.index(((a - DXY[slot][0]) % NX, (b - DXY[slot][1]) % NY))
            pieces.append(nrm[slot, :, theirs * rows:(theirs + 1) * rows])
        parts.append(jnp.concatenate(pieces, axis=1))
    high = parts[0]
    for part in parts[1:]:
        high = jnp.maximum(high, part)
    total = jnp.zeros((1, nq), f32)
    for part in parts:
        total += jnp.exp2(part - high)
    log_total = high + jnp.log2(total)
    for t in range(NZ):
        mk[t] = jnp.exp2(mk[t] - log_total)
    lsum = log_total[:, :rows] * math.log(2.0)

    def c_copy(t):
        return remote(cbuf.at[t], crecv.at[t], c_ss.at[t], c_rs.at[t], sibling)

    low, high = slice(0, HALF), slice(HALF, rows)
    moves = {
        5: (zsend.at[5], relay.at[0], 1, 5), 6: (zsend.at[6], relay.at[1], 2, 6),
        7: (zsend.at[7, low], relay_half.at[0], 3, 7), 8: (zsend.at[7, high], relay_half.at[1], 4, 8),
        1: (zsend.at[1], zrecv.at[2], 1, 2), 2: (zsend.at[2], zrecv.at[1], 2, 1),
        3: (zsend.at[3], zrecv.at[4], 3, 4), 4: (zsend.at[4], zrecv.at[3], 4, 3),
    }

    def z_copies(k):
        src, dst, peer, there = moves[k]
        return (
            remote(src, dst, z_ss.at[k], z_rs.at[there], z_peer(peer)),
            remote(zstep.at[k], zstepr.at[there], y_ss.at[k], y_rs.at[there], z_peer(peer)),
        )

    def z_send(k):
        for copy in z_copies(k):
            copy.start()

    def z_arrived(there):
        for k in moves:
            if moves[k][3] == there:
                for copy in z_copies(k):
                    copy.wait_recv()

    def combine(t):
        c_copy(t).wait_recv()
        both = own[t] + crecv[t]
        if t in (0, 3, 4):
            own[t] = both
        elif t == 7:
            for k, part in ((7, low), (8, high)):
                zsend[t, part], zstep[k] = quantized(both[part])
                z_send(k)
        else:
            zsend[t], zstep[t] = quantized(both)
            z_send(t)

    def line(way, d):
        return DXY.index((d, 0) if way == 0 else (0, d))

    def g_copies(way, d, e):
        k, there = 16 * way + 4 * d + e, 16 * way + 4 * ((4 - d) % 4) + e
        peer = plane_peer(line(way, d))
        return (
            remote(gsend.at[k], grecv.at[there], g_ss.at[k], g_rs.at[there], peer),
            remote(gstep.at[k], gstepr.at[there], i_ss.at[k], i_rs.at[there], peer),
        )

    def e_copies(way, d):
        k, there = 4 * way + d, 4 * way + (4 - d) % 4
        peer = plane_peer(line(1 - way, d))
        return (
            remote(esend.at[k], erecv.at[there], e_ss.at[k], e_rs.at[there], peer),
            remote(estep.at[k], estepr.at[there], j_ss.at[k], j_rs.at[there], peer),
        )

    def set_weights(t, g):
        lanes = slice(g * 256, (g + 1) * 256)
        e = es[t, :, lanes].reshape(2, 16, 8, 256) * mk[t, :, lanes]
        target = tg[t, :, lanes].reshape(2, 1, 8, 256)
        w = jnp.where(within == target, e - 1.0, e).reshape(256, 256).astype(bf16)
        wts[t * 256:(t + 1) * 256, lanes] = w

    def poi_step(t):
        grad = jnp.zeros((256, width), f32)
        for g in range(chunks):
            grad += jnp.dot(
                wts[t * 256:(t + 1) * 256, g * 256:(g + 1) * 256],
                qall[2 * g:2 * g + 2, :rows, :].reshape(256, width),
                preferred_element_type=f32,
            )
        own[t] = grad[:rows]
        cbuf[t] = grad[rows:]
        c_copy(t).start()

    def query_step(g):
        grad = jnp.dot(pt[...], wts[:, g * 256:(g + 1) * 256], preferred_element_type=f32)
        for half in range(2):
            slot = 2 * g + half
            piece = grad[:, half * rows:(half + 1) * rows]
            if slot < AXIS:
                qown[slot] = piece
            for way in range(2):
                d, e = DXY[slot] if way == 0 else DXY[slot][::-1]
                if d > 0:
                    k = 16 * way + 4 * d + e
                    gsend[k], gstep[k] = quantized(piece[way * rows:(way + 1) * rows])
                    for copy in g_copies(way, d, e):
                        copy.start()

    later = (1, 2, 3, 4, 0)

    def early(t):
        for g in range(chunks):
            set_weights(t, g)
        poi_step(t)

    def chunk(g):
        for t in later:
            set_weights(t, g)
        query_step(g)

    early(7)
    early(5)
    early(6)
    chunk(7)
    combine(7)
    combine(5)
    chunk(6)
    combine(6)
    for g in range(chunks - 3, -1, -1):
        chunk(g)
    for number, t in enumerate(later):
        poi_step(t)
        if number >= LAG:
            combine(later[number - LAG])
    for t in later[len(later) - LAG:]:
        combine(t)

    def decoded(v, step):
        return v.astype(jnp.int32).astype(f32) * step

    def add_line(way, e):
        mine = qown[line(1 - way, e), way * rows:(way + 1) * rows]
        for d in (1, 3, 2):
            for copy in g_copies(way, (4 - d) % 4, e):
                copy.wait_recv()
            k = 16 * way + 4 * d + e
            mine += decoded(grecv[k], gstepr[k])
        return mine

    def pass_line(way, e):
        k = 4 * way + e
        esend[k], estep[k] = quantized(add_line(way, e))
        for copy in e_copies(way, e):
            copy.start()

    for side_no, t in enumerate((3, 4)):
        z_arrived(5 + side_no)
        z_arrived(7 + side_no)
        both = own[t] + decoded(relay[side_no], zstepr[5 + side_no])
        half = decoded(relay_half[side_no], zstepr[7 + side_no])
        halves = [both[:HALF], both[HALF:]]
        halves[side_no] += half
        zsend[t], zstep[t] = quantized(jnp.concatenate(halves, axis=0))
        z_send(t)

    for e in (2, 1, 3):
        pass_line(0, e)
        pass_line(1, e)

    found = jnp.sum(ps[:, :rows], axis=0, keepdims=True)
    for slot in range(1, PLANE):
        s_copy(BACK[slot]).wait_recv()
        found += sidr[slot]
    loss_ref[...] = lsum - found * scale
    for way in range(2):
        grads = add_line(way, 0)
        for d in (2, 1, 3):
            for copy in e_copies(way, (4 - d) % 4):
                copy.wait_recv()
            grads += decoded(erecv[4 * way + d], estepr[4 * way + d])
        qg_ref[way * rows:(way + 1) * rows, :] = grads

    grads = own[0]
    for t in range(1, 5):
        z_arrived(t)
        grads += decoded(zrecv[t], zstepr[t])
    pg_ref[...] = grads

    for t in range(NZ):
        f_copy(t).wait_send()
        c_copy(t).wait_send()
        for copy in p_next(t):
            copy.wait_send()
    for k in moves:
        for copy in z_copies(k):
            copy.wait_send()
    for slot in range(1, PLANE):
        n_copy(slot).wait_send()
        s_copy(slot).wait_send()
    for way in range(2):
        for d in range(1, 4):
            for copy in e_copies(way, d):
                copy.wait_send()
            for e in range(4):
                for copy in g_copies(way, d, e):
                    copy.wait_send()
    for slot in range(1, AXIS):
        q_copy(slot).wait_send()
        for copy in pass_on(slot):
            copy.wait_send()


def finish(loss_ref, qt_ref, pg_ref, loss_out, qg_out, pg_out):
    scale = 1.0 / math.sqrt(pg_ref.shape[1])
    loss_out[...] = loss_ref[...]
    qg_out[...] = (qt_ref[...] * scale).T
    pg_out[...] = pg_ref[...] * scale


def body(queries, pois, query_region, block_region, region_mask, positive):
    rows, width = queries.shape
    regions = region_mask.shape[0]
    nq = PLANE * rows
    npoi = 2 * NZ * rows
    vmem = pl.BlockSpec(memory_space=pltpu.VMEM)
    hbm = pl.BlockSpec(memory_space=pl.ANY)
    dma = pltpu.SemaphoreType.DMA
    loss, query_grad, poi_grad = pl.pallas_call(
        kernel,
        out_shape=(
            jax.ShapeDtypeStruct((1, rows), f32),
            jax.ShapeDtypeStruct((width, rows), f32),
            jax.ShapeDtypeStruct((rows, width), f32),
        ),
        in_specs=[hbm, hbm, hbm, hbm, pl.BlockSpec(memory_space=pltpu.SMEM), hbm],
        out_specs=(vmem, vmem, vmem),
        scratch_shapes=[
            pltpu.VMEM((1, rows), jnp.int32),
            pltpu.VMEM((1, rows), jnp.int32),
            pltpu.VMEM((regions, regions), jnp.int32),
            dma((5,)),
            pltpu.VMEM((PLANE, EXT, width), bf16),
            pltpu.VMEM((2 * NZ, EXT, width), bf16),
            pltpu.VMEM((width, npoi), bf16),
            pltpu.VMEM((regions, nq), bf16),
            pltpu.VMEM((16 * NZ, regions), bf16),
            pltpu.VMEM((NZ, 16, nq), f32),
            pltpu.VMEM((NZ, 16, nq), f32),
            pltpu.VMEM((NZ, 2 * rows, nq), f32),
            pltpu.VMEM((npoi, nq), bf16),
            pltpu.VMEM((NZ, 8, nq), f32),
            pltpu.VMEM((NZ, 8, nq), f32),
            pltpu.VMEM((8, nq), f32),
            pltpu.VMEM((1, nq), f32),
            pltpu.VMEM((PLANE, 1, nq), f32),
            pltpu.VMEM((PLANE, 1, rows), f32),
            pltpu.VMEM((PLANE, 1, rows), f32),
            pltpu.VMEM((NZ, rows, width), f32),
            pltpu.VMEM((NZ, rows, width), f32),
            pltpu.VMEM((NZ, rows, width), f32),
            pltpu.VMEM((NZ, rows, width), jnp.int16),
            pltpu.VMEM((5, rows, width), jnp.int16),
            pltpu.VMEM((2, rows, width), jnp.int16),
            pltpu.VMEM((2, HALF, width), jnp.int16),
            pltpu.VMEM((NZ + 1, 1, width), f32),
            pltpu.VMEM((NZ + 1, 1, width), f32),
            pltpu.VMEM((AXIS, width, rows), f32),
            pltpu.VMEM((32, width // 2, rows), jnp.int16),
            pltpu.VMEM((32, width // 2, rows), jnp.int16),
            pltpu.VMEM((32, 1, rows), f32),
            pltpu.VMEM((32, 1, rows), f32),
            pltpu.VMEM((8, width // 2, rows), jnp.int16),
            pltpu.VMEM((8, width // 2, rows), jnp.int16),
            pltpu.VMEM((8, 1, rows), f32),
            pltpu.VMEM((8, 1, rows), f32),
            dma((PLANE,)), dma((PLANE,)), dma((2 * PLANE,)), dma((2 * PLANE,)), dma((NZ + 1,)), dma((NZ + 1,)),
            dma((NZ,)), dma((NZ,)), dma((PLANE,)), dma((PLANE,)), dma((PLANE,)), dma((PLANE,)),
            dma((NZ,)), dma((NZ,)), dma((NZ + 1,)), dma((NZ + 1,)), dma((NZ + 1,)), dma((NZ + 1,)),
            dma((32,)), dma((32,)), dma((32,)), dma((32,)), dma((8,)), dma((8,)), dma((8,)), dma((8,)),
        ],
        compiler_params=pltpu.CompilerParams(
            collective_id=0, has_side_effects=True, vmem_limit_bytes=56 * 2**20
        ),
    )(
        queries, pois, query_region.reshape(1, rows), positive.reshape(1, rows), block_region, region_mask
    )
    loss, query_grad, poi_grad = pl.pallas_call(
        finish,
        out_shape=(
            jax.ShapeDtypeStruct((1, rows), f32),
            jax.ShapeDtypeStruct((rows, width), f32),
            jax.ShapeDtypeStruct((rows, width), f32),
        ),
        in_specs=[vmem, vmem, vmem],
        out_specs=(vmem, vmem, vmem),
    )(loss, query_grad, poi_grad)
    return (loss.reshape(rows), query_grad, poi_grad)


def solution(mesh):
    in_specs = (
        P(("blk", "dp"), None),
        P(("blk", "dp"), None),
        P(("blk", "dp")),
        P(("blk", "dp")),
        P(),
        P(("blk", "dp")),
    )
    out_specs = (P(("blk", "dp")), P(("blk", "dp"), None), P(("blk", "dp"), None))
    return jax.shard_map(body, mesh=mesh, in_specs=in_specs, out_specs=out_specs, check_vma=False)
```

```python
import math

import jax
import jax.numpy as jnp
from jax import lax
from jax.experimental import pallas as pl
from jax.experimental.pallas import tpu as pltpu
from jax.sharding import PartitionSpec as P

MESH = pl.DeviceIdType.MESH
TILE = 128
EXT = 136
NX, NY, NZ = 4, 4, 8
PLANE = NX * NY
DZ = (0, 1, 7, 2, 6, 3, 5, 4)
ZBACK = tuple(DZ.index((NZ - d) % NZ) for d in DZ)
DXY = (
    (0, 0), (1, 0), (3, 0), (0, 1), (0, 3), (2, 0), (0, 2), (1, 1),
    (3, 3), (1, 3), (3, 1), (2, 1), (2, 3), (1, 2), (3, 2), (2, 2),
)
BACK = tuple(DXY.index(((NX - a) % NX, (NY - b) % NY)) for a, b in DXY)
AXIS = 7
HALF = 64
LAG = 2
CLOSED = -1e30
FLOOR = -1e29
TOP = 32767.0
NT = (((1,), (1,)), ((), ()))
f32, bf16 = jnp.float32, jnp.bfloat16


def quantized(v):
    top = jnp.max(jnp.abs(v.reshape(v.shape[0] // 8, 8, v.shape[1])), axis=0)
    top = jnp.max(top, axis=0, keepdims=True)
    step = jnp.where(top > 0.0, TOP / top, 0.0)
    return jnp.round(v * step).astype(jnp.int32).astype(jnp.int16), top * (1.0 / TOP)


def kernel(
    q_ref, p_ref, reg_ref, pos_ref, breg_ref, mask_ref,
    loss_ref, qg_ref, pg_ref,
    regs, poss, masks, l_ss, qall, pall, pt, hot, pick, tg, bias, es, wts, mk, lk, ps, st, nrm, side, sidr,
    own, cbuf, crecv, zsend, zrecv, relay, relay_half, zstep, zstepr, qown, gsend, grecv, gstep, gstepr, esend, erecv, estep, estepr,
    q_ss, q_rs, h_ss, h_rs, p_ss, p_rs, f_ss, f_rs, n_ss, n_rs, s_ss, s_rs,
    c_ss, c_rs, z_ss, z_rs, y_ss, y_rs, g_ss, g_rs, i_ss, i_rs, e_ss, e_rs, j_ss, j_rs,
):
    blk = lax.axis_index("blk")
    dp = lax.axis_index("dp")
    core = blk % 2
    y = blk // 4
    x = dp % NX
    z = (dp // NX) * 2 + (blk // 2) % 2
    width = q_ref.shape[1]
    rows = q_ref.shape[0]
    nq = PLANE * rows
    scale = 1.0 / math.sqrt(width)

    def device(xx, yy, zz, cc):
        return (yy * 4 + (zz % 2) * 2 + cc, (zz // 2) * NX + xx)

    def plane_peer(slot):
        return device((x + DXY[slot][0]) % NX, (y + DXY[slot][1]) % NY, z, core)

    def z_peer(t):
        return device(x, y, (z + DZ[t]) % NZ, core)

    sibling = device(x, y, z, 1 - core)

    def remote(src, dst, ss, rs, dev):
        return pltpu.make_async_remote_copy(
            src_ref=src, dst_ref=dst, send_sem=ss, recv_sem=rs, device_id=dev, device_id_type=MESH
        )

    loads = [
        pltpu.make_async_copy(src, dst, l_ss.at[k])
        for k, (src, dst) in enumerate((
            (reg_ref, regs), (pos_ref, poss), (mask_ref, masks),
            (q_ref, qall.at[0, :rows, :]), (p_ref, pall.at[0, :rows, :]),
        ))
    ]
    for load in loads:
        load.start()
    barrier = pltpu.get_barrier_semaphore()
    near = [plane_peer(slot) for slot in range(1, PLANE)] + [z_peer(t) for t in range(1, 5)] + [sibling]
    for peer in near:
        pl.semaphore_signal(barrier, inc=1, device_id=peer, device_id_type=MESH)

    for load in loads:
        load.wait()
    row = lax.broadcasted_iota(jnp.int32, (EXT - rows, rows), 0)
    pos = poss[...]
    small = jnp.where(row == 0, regs[...], jnp.where(row == 1, pos // TILE, pos % TILE)).astype(f32)
    small = small.astype(bf16)
    qall[0, rows:, :rows] = small
    qall[0, rows:, rows:] = small
    pall[0, rows:, :] = jnp.full((EXT - rows, width), breg_ref[0], jnp.int32).astype(f32).astype(bf16)

    pl.semaphore_wait(barrier, len(near))

    def q_copy(slot):
        return remote(qall.at[0], qall.at[BACK[slot]], q_ss.at[slot], q_rs.at[BACK[slot]], plane_peer(slot))

    def h_copy(slot, peer):
        a, b = DXY[slot]
        c, d = DXY[peer]
        there = DXY.index(((a - c) % NX, (b - d) % NY))
        part = slice(0, HALF) if b == 0 else slice(HALF, EXT)
        k = 2 * there + (0 if b == 0 else 1)
        return remote(qall.at[slot, part], qall.at[there, part], h_ss.at[k], h_rs.at[k], plane_peer(peer))

    def pass_on(slot):
        a, b = DXY[slot]
        return [h_copy(slot, DXY.index((0, d) if b == 0 else (d, 0))) for d in (1, 3, 2)]

    def p_copy(slot, part, t, k, dz):
        return remote(pall.at[2 * slot, part], pall.at[2 * t, part], p_ss.at[k], p_rs.at[k], z_peer(DZ.index(dz)))

    def p_next(t):
        whole, low, high = slice(0, EXT), slice(0, HALF), slice(HALF, EXT)
        if t == 0:
            return [p_copy(0, whole, ZBACK[k], ZBACK[k], DZ[k]) for k in (3, 4, 1, 2)]
        if DZ[t] == 2:
            return [p_copy(t, low, 7, 7, NZ - 2), p_copy(t, whole, 5, 5, NZ - 1)]
        if DZ[t] == 6:
            return [p_copy(t, high, 7, 8, 2), p_copy(t, whole, 6, 6, 1)]
        return []

    def p_wait(t):
        if t < 7:
            p_copy(0, slice(0, EXT), t, t, 1).wait_recv()
        else:
            p_copy(0, slice(0, HALF), 7, 7, 1).wait_recv()
            p_copy(0, slice(HALF, EXT), 7, 8, 1).wait_recv()

    def f_copy(t):
        return remote(pall.at[2 * t], pall.at[2 * t + 1], f_ss.at[t], f_rs.at[t], sibling)

    for copy in p_next(0):
        copy.start()
    for slot in range(1, AXIS):
        q_copy(slot).start()
    f_copy(0).start()

    ps[...] = jnp.zeros_like(ps)
    region_mask = masks[...].astype(f32).astype(bf16)
    regions = region_mask.shape[0]
    region_ids = lax.broadcasted_iota(jnp.int32, (regions, rows), 0).astype(f32)
    lane_ids = lax.broadcasted_iota(jnp.int32, (8, regions), 1).astype(f32)
    within = lax.broadcasted_iota(jnp.int32, (2 * rows, 256), 0) % rows
    within = within.astype(f32).reshape(2, 16, 8, 256)
    starts = []
    for t in range(NZ):
        for cc in (core, 1 - core):
            b, d = device(x, y, (z + DZ[t]) % NZ, cc)
            starts.append(((b * 16 + d) * TILE).astype(f32))

    def take_queries(slot):
        extra = qall[slot, rows:, :rows].astype(f32)
        lanes = slice(slot * rows, (slot + 1) * rows)
        hot[:, lanes] = (region_ids == extra[0:1]).astype(f32).astype(bf16)
        target = jnp.broadcast_to(extra[1:2] * TILE + extra[2:3], (8, rows))
        for k, start in enumerate(starts):
            tg[k // 2, 8 * (k % 2):8 * (k % 2) + 8, lanes] = target - start

    def take_pair(t):
        pair = pall[2 * t:2 * t + 2, :rows, :].reshape(256, width)
        pt[:, t * 256:(t + 1) * 256] = pair.T
        hots = [
            (lane_ids == pall[2 * t + h, rows:rows + 8, :regions].astype(f32)).astype(f32)
            for h in range(2)
        ]
        pick[16 * t:16 * t + 16, :] = lax.dot_general(
            jnp.concatenate(hots, axis=0).astype(bf16), region_mask, NT, preferred_element_type=f32
        ).astype(bf16)

    def set_bias(first, last, lanes):
        opened = jnp.dot(pick[16 * first:16 * last, :], hot[:, lanes], preferred_element_type=f32)
        for t in range(first, last):
            at = tg[t, :, lanes]
            part = (opened[16 * (t - first):16 * (t - first) + 16] > 0.5) | ((at >= 0.0) & (at < TILE))
            bias[t, :, lanes] = jnp.where(part, 0.0, CLOSED)

    log2e_scale = scale / math.log(2.0)

    def score_tile(t, g):
        lanes = slice(g * 256, (g + 1) * 256)
        pair = pall[2 * t:2 * t + 2, :rows, :].reshape(256, width)
        qg = qall[2 * g:2 * g + 2, :rows, :].reshape(256, width)
        s = lax.dot_general(pair, qg, NT, preferred_element_type=f32).reshape(2, 16, 8, 256)
        target = tg[t, :, lanes].reshape(2, 1, 8, 256)
        ps[:, lanes] += jnp.sum(jnp.where(within == target, s, 0.0), axis=(0, 1))
        s = s * log2e_scale + bias[t, :, lanes].reshape(2, 1, 8, 256)
        high = jnp.max(jnp.max(s, axis=(0, 1)), axis=0, keepdims=True)
        high = jnp.broadcast_to(jnp.maximum(high, FLOOR), (8, 256))
        mk[t, :, lanes] = high
        e = jnp.exp2(s - high)
        lk[t, :, lanes] = jnp.sum(e, axis=(0, 1))
        es[t, :, lanes] = e.reshape(256, 256)

    chunks = nq // 256
    ready = {"t": 0, "g": 0}

    def arrived_queries(slot):
        if slot > 0:
            q_copy(BACK[slot]).wait_recv()
            for copy in pass_on(slot):
                copy.start()
        take_queries(slot)

    def arrived_shard(t):
        p_wait(t)
        for copy in p_next(t):
            copy.start()
        f_copy(t).start()

    def use_pair(t):
        f_copy(t).wait_recv()
        take_pair(t)
        ready["t"] = t + 1
        if ready["g"]:
            set_bias(t, t + 1, slice(0, ready["g"] * 256))
        for g in range(ready["g"]):
            score_tile(t, g)

    def use_chunk(g):
        for slot in (2 * g, 2 * g + 1):
            if slot >= AXIS:
                for half in range(2):
                    part = slice(0, HALF) if half == 0 else slice(HALF, EXT)
                    k = 2 * slot + half
                    remote(qall.at[slot, part], qall.at[slot, part], h_ss.at[k], h_rs.at[k], sibling).wait_recv()
                take_queries(slot)
        ready["g"] = g + 1
        if ready["t"]:
            set_bias(0, ready["t"], slice(g * 256, (g + 1) * 256))
        for t in range(ready["t"]):
            score_tile(t, g)

    steps = (
        (arrived_queries, (0, 1, 2, 3, 4)), (arrived_shard, (3, 4)), (arrived_queries, (5, 6)), (arrived_shard, (1, 2)),
        (use_pair, (0,)), (use_chunk, (0, 1, 2)), (use_pair, (1, 2, 3, 4)), (use_chunk, (3, 4)),
        (arrived_shard, (5, 6)), (use_chunk, (5,)), (arrived_shard, (7,)), (use_pair, (5, 6)), (use_chunk, (6, 7)),
        (use_pair, (7,)),
    )
    for step, items in steps:
        for item in items:
            step(item)

    high = mk[0]
    for t in range(1, NZ):
        high = jnp.maximum(high, mk[t])
    total = jnp.zeros((8, nq), f32)
    for t in range(NZ):
        total += lk[t] * jnp.exp2(mk[t] - high)
    total = jnp.sum(total, axis=0, keepdims=True)
    st[...] = jnp.where(total > 0.0, high[0:1] + jnp.log2(jnp.where(total > 0.0, total, 1.0)), CLOSED)

    def n_copy(slot):
        return remote(st, nrm.at[BACK[slot]], n_ss.at[slot], n_rs.at[BACK[slot]], plane_peer(slot))

    def s_copy(slot):
        return remote(side.at[slot], sidr.at[BACK[slot]], s_ss.at[slot], s_rs.at[BACK[slot]], plane_peer(slot))

    for slot in range(PLANE - 1, 0, -1):
        n_copy(slot).start()
    for slot in range(PLANE - 1, 0, -1):
        side[slot] = jnp.sum(ps[:, slot * rows:(slot + 1) * rows], axis=0, keepdims=True)
        s_copy(slot).start()
    parts = [st[...]]
    for slot in range(1, PLANE):
        n_copy(BACK[slot]).wait_recv()
        pieces = []
        for a, b in DXY:
            theirs = DXY.index(((a - DXY[slot][0]) % NX, (b - DXY[slot][1]) % NY))
            pieces.append(nrm[slot, :, theirs * rows:(theirs + 1) * rows])
        parts.append(jnp.concatenate(pieces, axis=1))
    high = parts[0]
    for part in parts[1:]:
        high = jnp.maximum(high, part)
    total = jnp.zeros((1, nq), f32)
    for part in parts:
        total += jnp.exp2(part - high)
    log_total = high + jnp.log2(total)
    for t in range(NZ):
        mk[t] = jnp.exp2(mk[t] - log_total)
    lsum = log_total[:, :rows] * math.log(2.0)

    def c_copy(t):
        return remote(cbuf.at[t], crecv.at[t], c_ss.at[t], c_rs.at[t], sibling)

    low, high = slice(0, HALF), slice(HALF, rows)
    moves = {
        5: (zsend.at[5], relay.at[0], 1, 5), 6: (zsend.at[6], relay.at[1], 2, 6),
        7: (zsend.at[7, low], relay_half.at[0], 3, 7), 8: (zsend.at[7, high], relay_half.at[1], 4, 8),
        1: (zsend.at[1], zrecv.at[2], 1, 2), 2: (zsend.at[2], zrecv.at[1], 2, 1),
        3: (zsend.at[3], zrecv.at[4], 3, 4), 4: (zsend.at[4], zrecv.at[3], 4, 3),
    }

    def z_copies(k):
        src, dst, peer, there = moves[k]
        return (
            remote(src, dst, z_ss.at[k], z_rs.at[there], z_peer(peer)),
            remote(zstep.at[k], zstepr.at[there], y_ss.at[k], y_rs.at[there], z_peer(peer)),
        )

    def z_send(k):
        for copy in z_copies(k):
            copy.start()

    def z_arrived(there):
        for k in moves:
            if moves[k][3] == there:
                for copy in z_copies(k):
                    copy.wait_recv()

    def combine(t):
        c_copy(t).wait_recv()
        both = own[t] + crecv[t]
        if t in (0, 3, 4):
            own[t] = both
        elif t == 7:
            for k, part in ((7, low), (8, high)):
                zsend[t, part], zstep[k] = quantized(both[part])
                z_send(k)
        else:
            zsend[t], zstep[t] = quantized(both)
            z_send(t)

    def line(way, d):
        return DXY.index((d, 0) if way == 0 else (0, d))

    def g_copies(way, d, e):
        k, there = 16 * way + 4 * d + e, 16 * way + 4 * ((4 - d) % 4) + e
        peer = plane_peer(line(way, d))
        return (
            remote(gsend.at[k], grecv.at[there], g_ss.at[k], g_rs.at[there], peer),
            remote(gstep.at[k], gstepr.at[there], i_ss.at[k], i_rs.at[there], peer),
        )

    def e_copies(way, d):
        k, there = 4 * way + d, 4 * way + (4 - d) % 4
        peer = plane_peer(line(1 - way, d))
        return (
            remote(esend.at[k], erecv.at[there], e_ss.at[k], e_rs.at[there], peer),
            remote(estep.at[k], estepr.at[there], j_ss.at[k], j_rs.at[there], peer),
        )

    def set_weights(t, g):
        lanes = slice(g * 256, (g + 1) * 256)
        e = es[t, :, lanes].reshape(2, 16, 8, 256) * mk[t, :, lanes]
        target = tg[t, :, lanes].reshape(2, 1, 8, 256)
        w = jnp.where(within == target, e - 1.0, e).reshape(256, 256).astype(bf16)
        wts[t * 256:(t + 1) * 256, lanes] = w

    def poi_step(t):
        grad = jnp.zeros((256, width), f32)
        for g in range(chunks):
            grad += jnp.dot(
                wts[t * 256:(t + 1) * 256, g * 256:(g + 1) * 256],
                qall[2 * g:2 * g + 2, :rows, :].reshape(256, width),
                preferred_element_type=f32,
            )
        own[t] = grad[:rows]
        cbuf[t] = grad[rows:]
        c_copy(t).start()

    def query_step(g):
        grad = jnp.dot(pt[...], wts[:, g * 256:(g + 1) * 256], preferred_element_type=f32)
        for half in range(2):
            slot = 2 * g + half
            piece = grad[:, half * rows:(half + 1) * rows]
            if slot < AXIS:
                qown[slot] = piece
            for way in range(2):
                d, e = DXY[slot] if way == 0 else DXY[slot][::-1]
                if d > 0:
                    k = 16 * way + 4 * d + e
                    gsend[k], gstep[k] = quantized(piece[way * rows:(way + 1) * rows])
                    for copy in g_copies(way, d, e):
                        copy.start()

    later = (1, 3, 4, 2, 0)

    def early(t):
        for g in range(chunks):
            set_weights(t, g)
        poi_step(t)

    def chunk(g):
        for t in later:
            set_weights(t, g)
        query_step(g)

    early(7)
    early(5)
    early(6)
    chunk(7)
    combine(7)
    combine(5)
    chunk(6)
    combine(6)
    for g in range(chunks - 3, -1, -1):
        chunk(g)
    for number, t in enumerate(later):
        poi_step(t)
        if number >= LAG:
            combine(later[number - LAG])
    combine(2)

    def decoded(v, step):
        return v.astype(jnp.int32).astype(f32) * step

    def add_line(way, e):
        mine = qown[line(1 - way, e), way * rows:(way + 1) * rows]
        for d in (1, 3, 2):
            for copy in g_copies(way, (4 - d) % 4, e):
                copy.wait_recv()
            k = 16 * way + 4 * d + e
            mine += decoded(grecv[k], gstepr[k])
        return mine

    def pass_line(way, e):
        k = 4 * way + e
        esend[k], estep[k] = quantized(add_line(way, e))
        for copy in e_copies(way, e):
            copy.start()

    for side_no, t in enumerate((3, 4)):
        z_arrived(5 + side_no)
        z_arrived(7 + side_no)
        both = own[t] + decoded(relay[side_no], zstepr[5 + side_no])
        half = decoded(relay_half[side_no], zstepr[7 + side_no])
        halves = [both[:HALF], both[HALF:]]
        halves[side_no] += half
        zsend[t], zstep[t] = quantized(jnp.concatenate(halves, axis=0))
        z_send(t)

    combine(0)
    for e in (2, 1, 3):
        pass_line(0, e)
        pass_line(1, e)

    found = jnp.sum(ps[:, :rows], axis=0, keepdims=True)
    for slot in range(1, PLANE):
        s_copy(BACK[slot]).wait_recv()
        found += sidr[slot]
    loss_ref[...] = lsum - found * scale
    for way in range(2):
        grads = add_line(way, 0)
        for d in (2, 1, 3):
            for copy in e_copies(way, (4 - d) % 4):
                copy.wait_recv()
            grads += decoded(erecv[4 * way + d], estepr[4 * way + d])
        qg_ref[way * rows:(way + 1) * rows, :] = grads

    grads = own[0]
    for t in range(1, 5):
        z_arrived(t)
        grads += decoded(zrecv[t], zstepr[t])
    pg_ref[...] = grads

    for t in range(NZ):
        f_copy(t).wait_send()
        c_copy(t).wait_send()
        for copy in p_next(t):
            copy.wait_send()
    for k in moves:
        for copy in z_copies(k):
            copy.wait_send()
    for slot in range(1, PLANE):
        n_copy(slot).wait_send()
        s_copy(slot).wait_send()
    for way in range(2):
        for d in range(1, 4):
            for copy in e_copies(way, d):
                copy.wait_send()
            for e in range(4):
                for copy in g_copies(way, d, e):
                    copy.wait_send()
    for slot in range(1, AXIS):
        q_copy(slot).wait_send()
        for copy in pass_on(slot):
            copy.wait_send()


def finish(loss_ref, qt_ref, pg_ref, loss_out, qg_out, pg_out):
    scale = 1.0 / math.sqrt(pg_ref.shape[1])
    loss_out[...] = loss_ref[...]
    qg_out[...] = (qt_ref[...] * scale).T
    pg_out[...] = pg_ref[...] * scale


def body(queries, pois, query_region, block_region, region_mask, positive):
    rows, width = queries.shape
    regions = region_mask.shape[0]
    nq = PLANE * rows
    npoi = 2 * NZ * rows
    vmem = pl.BlockSpec(memory_space=pltpu.VMEM)
    hbm = pl.BlockSpec(memory_space=pl.ANY)
    dma = pltpu.SemaphoreType.DMA
    loss, query_grad, poi_grad = pl.pallas_call(
        kernel,
        out_shape=(
            jax.ShapeDtypeStruct((1, rows), f32),
            jax.ShapeDtypeStruct((width, rows), f32),
            jax.ShapeDtypeStruct((rows, width), f32),
        ),
        in_specs=[hbm, hbm, hbm, hbm, pl.BlockSpec(memory_space=pltpu.SMEM), hbm],
        out_specs=(vmem, vmem, vmem),
        scratch_shapes=[
            pltpu.VMEM((1, rows), jnp.int32),
            pltpu.VMEM((1, rows), jnp.int32),
            pltpu.VMEM((regions, regions), jnp.int32),
            dma((5,)),
            pltpu.VMEM((PLANE, EXT, width), bf16),
            pltpu.VMEM((2 * NZ, EXT, width), bf16),
            pltpu.VMEM((width, npoi), bf16),
            pltpu.VMEM((regions, nq), bf16),
            pltpu.VMEM((16 * NZ, regions), bf16),
            pltpu.VMEM((NZ, 16, nq), f32),
            pltpu.VMEM((NZ, 16, nq), f32),
            pltpu.VMEM((NZ, 2 * rows, nq), f32),
            pltpu.VMEM((npoi, nq), bf16),
            pltpu.VMEM((NZ, 8, nq), f32),
            pltpu.VMEM((NZ, 8, nq), f32),
            pltpu.VMEM((8, nq), f32),
            pltpu.VMEM((1, nq), f32),
            pltpu.VMEM((PLANE, 1, nq), f32),
            pltpu.VMEM((PLANE, 1, rows), f32),
            pltpu.VMEM((PLANE, 1, rows), f32),
            pltpu.VMEM((NZ, rows, width), f32),
            pltpu.VMEM((NZ, rows, width), f32),
            pltpu.VMEM((NZ, rows, width), f32),
            pltpu.VMEM((NZ, rows, width), jnp.int16),
            pltpu.VMEM((5, rows, width), jnp.int16),
            pltpu.VMEM((2, rows, width), jnp.int16),
            pltpu.VMEM((2, HALF, width), jnp.int16),
            pltpu.VMEM((NZ + 1, 1, width), f32),
            pltpu.VMEM((NZ + 1, 1, width), f32),
            pltpu.VMEM((AXIS, width, rows), f32),
            pltpu.VMEM((32, width // 2, rows), jnp.int16),
            pltpu.VMEM((32, width // 2, rows), jnp.int16),
            pltpu.VMEM((32, 1, rows), f32),
            pltpu.VMEM((32, 1, rows), f32),
            pltpu.VMEM((8, width // 2, rows), jnp.int16),
            pltpu.VMEM((8, width // 2, rows), jnp.int16),
            pltpu.VMEM((8, 1, rows), f32),
            pltpu.VMEM((8, 1, rows), f32),
            dma((PLANE,)), dma((PLANE,)), dma((2 * PLANE,)), dma((2 * PLANE,)), dma((NZ + 1,)), dma((NZ + 1,)),
            dma((NZ,)), dma((NZ,)), dma((PLANE,)), dma((PLANE,)), dma((PLANE,)), dma((PLANE,)),
            dma((NZ,)), dma((NZ,)), dma((NZ + 1,)), dma((NZ + 1,)), dma((NZ + 1,)), dma((NZ + 1,)),
            dma((32,)), dma((32,)), dma((32,)), dma((32,)), dma((8,)), dma((8,)), dma((8,)), dma((8,)),
        ],
        compiler_params=pltpu.CompilerParams(
            collective_id=0, has_side_effects=True, vmem_limit_bytes=56 * 2**20
        ),
    )(
        queries, pois, query_region.reshape(1, rows), positive.reshape(1, rows), block_region, region_mask
    )
    loss, query_grad, poi_grad = pl.pallas_call(
        finish,
        out_shape=(
            jax.ShapeDtypeStruct((1, rows), f32),
            jax.ShapeDtypeStruct((rows, width), f32),
            jax.ShapeDtypeStruct((rows, width), f32),
        ),
        in_specs=[vmem, vmem, vmem],
        out_specs=(vmem, vmem, vmem),
    )(loss, query_grad, poi_grad)
    return (loss.reshape(rows), query_grad, poi_grad)


def solution(mesh):
    in_specs = (
        P(("blk", "dp"), None),
        P(("blk", "dp"), None),
        P(("blk", "dp")),
        P(("blk", "dp")),
        P(),
        P(("blk", "dp")),
    )
    out_specs = (P(("blk", "dp")), P(("blk", "dp"), None), P(("blk", "dp"), None))
    return jax.shard_map(body, mesh=mesh, in_specs=in_specs, out_specs=out_specs, check_vma=False)
```
